32 devices in a mesh: grp: 2 (over y), ctx: 4 (over z), mdl: 2 (over x), sub: 2 (over core).
Axes of the slice: x: 2, y: 2, z: 4, core: 2. Of those that a mesh axis runs over, the one named last changes fastest.
Arguments:
- queries: bfloat16 [512, 8192], P(('grp', 'ctx'), ('mdl', 'sub')), parts along dimension 0, may hold values from -6 to 6
- cache_slots: bfloat16 [16384, 8, 256], P(('grp', 'ctx'), ('mdl', 'sub')), parts along dimension 0, may hold values from -8 to 8
- slot_position: int32 [16384], P(('grp', 'ctx')), parts along dimension 0, may hold values from 0 to 8191, as said below
- shard_fill: int32 [8], P(('grp', 'ctx')), parts along dimension 0, may hold values from 1024 to 2048, as said below
- image_end: int32 [4], P('grp'), parts along dimension 0, may hold values from 2048 to 8191
- residual: bfloat16 [512, 8192], P(('grp', 'mdl', 'sub'), 'ctx'), parts along dimension 0, may hold values from -11 to 11
- out_weight: bfloat16 [8192, 8192], P(('mdl', 'sub'), 'ctx'), may hold values from -0.0625 to 0.0625
- gate_weight: bfloat16 [8192, 28672], P('ctx', ('mdl', 'sub')), may hold values from -0.0625 to 0.0625
- up_weight: bfloat16 [8192, 28672], P('ctx', ('mdl', 'sub')), may hold values from -0.0625 to 0.0625
- down_weight: bfloat16 [28672, 8192], P(('mdl', 'sub'), 'ctx'), may hold values from -0.03125 to 0.03125
Outputs:
- attended: float32 [512, 8192], P(('grp', 'mdl', 'sub'), 'ctx'), parts along dimension 0
- forward_delta: float32 [512, 8192], P(('grp', 'mdl', 'sub'), 'ctx'), parts along dimension 0
The draws below stay inside these ranges and needn't reach their ends.
There are 2 independent parts, one for each index of `grp`. The reference program is written for one: setup_inputs(seed, part) draws one part's arguments, and reference() takes and returns one part's arrays. A program takes and returns all parts, laid end to end along the dimension named above; an argument that names none is the same for every part. Nothing has to cross between parts.
Inputs may be any that keep to these rules, and one draw needn't show every extreme that they name: `slot_position`: each position appears in exactly one slot. `shard_fill`: some shard is full.
All inputs are finite; a program needn't handle non-finite values.
Results may differ from the reference program's by a relative error of at most 0.012.
Values may be sent and summed in bfloat16 or wider, within the bound.
A program may use at most 256 MiB of HBM per device.

```python
import jax
import jax.numpy as jnp
from jax import lax

D = 8192
FF = 28672
HQ = 64
KVH = 8
HD = 128
IMAGES = 2
IMG_TOK = 128
CTX_DEV = 2048
QTOK = 256
CACHE = 8192


def draw_queries(key, part):
    base_draw = jnp.clip(jax.random.normal(jax.random.fold_in(key, 1), (QTOK, HQ * HD), jnp.float32), -6.0, 6.0)
    return base_draw.astype(jnp.bfloat16)


def draw_cache_slots(key, part):
    shard_count = CACHE // CTX_DEV
    keys_part = jnp.clip(jax.random.normal(jax.random.fold_in(key, 2), (CACHE, KVH, HD), jnp.float32), -6.0, 6.0)
    offsets = jax.random.normal(jax.random.fold_in(key, 3), (shard_count, KVH, HD), jnp.float32)
    noise = jax.random.normal(jax.random.fold_in(key, 4), (CACHE, KVH, HD), jnp.float32)
    values_part = jnp.clip(noise + 1.5 * jnp.repeat(offsets, CTX_DEV, axis=0), -8.0, 8.0)
    return jnp.concatenate([keys_part, values_part], axis=2).astype(jnp.bfloat16)


def draw_slot_position(key, part):
    shard_count = CACHE // CTX_DEV
    base_draw = jnp.broadcast_to(jnp.arange(shard_count, dtype=jnp.int32)[None, :], (CTX_DEV, shard_count))
    mixed = jax.random.permutation(jax.random.fold_in(key, 5), base_draw, axis=1, independent=True)
    positions = jnp.arange(CTX_DEV, dtype=jnp.int32)[:, None] * shard_count + mixed
    return positions.T.reshape(CACHE).astype(jnp.int32)


def draw_shard_fill(key, part):
    shard_count = CACHE // CTX_DEV
    fill_draw = jax.random.randint(jax.random.fold_in(key, 6), (shard_count,), CTX_DEV // 2, CTX_DEV + 1)
    full_shard = jax.random.randint(jax.random.fold_in(key, 7), (), 0, shard_count)
    return jnp.where(jnp.arange(shard_count) == full_shard, CTX_DEV, fill_draw).astype(jnp.int32)


def draw_residual(key, part):
    base_draw = jnp.clip(jax.random.normal(jax.random.fold_in(key, 8), (QTOK, D), jnp.float32), -4.0, 4.0)
    column_index = jnp.arange(D).astype(jnp.float32) / D
    column_scale = 0.3 * jnp.power(3.0, column_index)
    return (base_draw * column_scale[None, :]).astype(jnp.bfloat16)


def shard_levels(stream_key, extent, split, low, largest):
    gain, own = 1.0, jax.random.fold_in(stream_key, 6)
    for axis_at, parts in split:
        draws = jnp.exp(jax.random.uniform(jax.random.fold_in(own, axis_at), (parts,), jnp.float32, low / len(split), largest / len(split)))
        gain = gain * jnp.repeat(draws, extent[axis_at] // parts).reshape([-1 if axis == axis_at else 1 for axis in range(len(extent))])
    return gain


def scatter_about(stream_key, extent, spread, reach, split=(), kind=jnp.bfloat16):
    loudness = shard_levels(stream_key, extent, split, -0.22, 0.18) if split else 1.0
    result = jax.random.normal(stream_key, extent, jnp.float32) * spread * loudness
    return jnp.minimum(jnp.maximum(result, -reach), reach).astype(kind)


def setup_inputs(seed: int = 0, part: int = 0) -> dict:
    keys = jax.random.split(jax.random.key(seed), 11)
    own_keys = jax.random.split(jax.random.fold_in(keys[10], part), 11)
    return {
        "queries": draw_queries(jax.random.fold_in(jax.random.fold_in(keys[10], part), 71), part),
        "cache_slots": draw_cache_slots(jax.random.fold_in(jax.random.fold_in(keys[10], part), 71), part),
        "slot_position": draw_slot_position(jax.random.fold_in(jax.random.fold_in(keys[10], part), 71), part),
        "shard_fill": draw_shard_fill(jax.random.fold_in(jax.random.fold_in(keys[10], part), 71), part),
        "image_end": jax.random.randint(own_keys[4], (IMAGES,), CACHE // 4, CACHE).astype(jnp.int32),
        "residual": draw_residual(jax.random.fold_in(jax.random.fold_in(keys[10], part), 71), part),
        "out_weight": scatter_about(keys[6], (HQ * HD, D), (HQ * HD) ** -0.5, 0.0625, ((0, 4), (1, 4))),
        "gate_weight": scatter_about(keys[7], (D, FF), D ** -0.5, 0.0625, ((0, 4), (1, 4))),
        "up_weight": scatter_about(keys[8], (D, FF), D ** -0.5, 0.0625, ((0, 4), (1, 4))),
        "down_weight": scatter_about(keys[9], (FF, D), FF ** -0.5, 0.03125, ((0, 4), (1, 4))),
    }


def reference(queries, cache_slots, slot_position, shard_fill, image_end, residual, out_weight, gate_weight, up_weight, down_weight):
    slot_index = jnp.arange(CACHE, dtype=jnp.int32)
    owner_shard = slot_index // CTX_DEV
    fill_count = shard_fill[owner_shard]
    slot_tags = jnp.where(slot_index % CTX_DEV < fill_count, slot_position, 2 ** 30).astype(jnp.int32)
    row_index = jnp.arange(QTOK, dtype=jnp.int32)
    limits = image_end[row_index // IMG_TOK]
    visible = slot_tags[None, :] <= limits[:, None]
    group_size = HQ // KVH
    score_scale = HD ** (-0.5)

    def one_head(head_index):
        query_part = lax.dynamic_slice_in_dim(queries, head_index * HD, HD, 1)
        head_cache = lax.dynamic_index_in_dim(cache_slots, head_index // group_size, 1, keepdims=False)
        key_part = head_cache[:, :HD]
        value_part = head_cache[:, HD:]
        scores = jnp.dot(query_part, key_part.T, preferred_element_type=jnp.float32) * score_scale
        masked = jnp.where(visible, scores, -1e+30)
        row_max = lax.optimization_barrier(jnp.max(masked, axis=1))
        expo = jnp.where(visible, jnp.exp(masked - row_max[:, None]), 0.0)
        totals = lax.optimization_barrier(jnp.sum(expo, axis=1))
        attn_prob = expo.astype(jnp.bfloat16)
        weighted = jnp.dot(attn_prob, value_part, preferred_element_type=jnp.float32)
        return (weighted / totals[:, None]).astype(jnp.bfloat16)
    per_head = lax.map(one_head, jnp.arange(HQ, dtype=jnp.int32))
    attention = jnp.transpose(per_head, (1, 0, 2)).reshape(QTOK, HQ * HD)
    hidden_state = residual.astype(jnp.float32) + jnp.dot(attention, out_weight, preferred_element_type=jnp.float32)
    attended = hidden_state
    square_mean = lax.optimization_barrier(jnp.sum(hidden_state * hidden_state, axis=1)) / D
    normed = (hidden_state * lax.rsqrt(square_mean + 1e-05)[:, None]).astype(jnp.bfloat16)
    gate = jnp.dot(normed, gate_weight, preferred_element_type=jnp.float32)
    up_value = jnp.dot(normed, up_weight, preferred_element_type=jnp.float32)
    hidden = (jax.nn.silu(gate) * up_value).astype(jnp.bfloat16)
    forward_delta = jnp.dot(hidden, down_weight, preferred_element_type=jnp.float32)
    return (attended, forward_delta)
```

```python
import functools

import jax
import jax.numpy as jnp
from jax import lax
from jax.experimental import pallas as pl
from jax.experimental.pallas import tpu as pltpu
from jax.sharding import PartitionSpec as P

D = 8192
IMAGES = 2
IMG_TOK = 128
LOG2_E = 1.4426950408889634


def visible_limits(image_end, first_row, query_count):
    row_index = first_row + jnp.arange(query_count, dtype=jnp.int32)
    image_index = row_index // IMG_TOK
    matches = image_index[:, None] == jnp.arange(IMAGES, dtype=jnp.int32)[None, :]
    return jnp.sum(jnp.where(matches, image_end[None, :], 0), axis=1)


MESH = pl.DeviceIdType.MESH
LAG = 3


def ffn_kernel(
    n, nm, lag, x_ref, gate_hbm, up_hbm, down_hbm, out_ref,
    own, sum_lo, sum_hi, hid, gate_buf, up_buf, down_buf, acc, pair_out, pair_in, cross_out, cross_in,
    gate_sem, up_sem, down_sem,
    lo_send, lo_recv, hi_send, hi_recv, hlo_send, hlo_recv, hhi_send, hhi_recv,
    pair_send, pair_recv, cross_send, cross_recv,
):
    c = lax.axis_index("ctx")
    m = lax.axis_index("mdl")
    s = lax.axis_index("sub")
    chunks = own.shape[0]
    rows = x_ref.shape[0]
    half = rows // 2
    width = hid.shape[2]
    depth = gate_buf.shape[0]

    barrier = pltpu.get_barrier_semaphore()
    for by in (1, n - 1):
        pl.semaphore_signal(barrier, inc=1, device_id={"ctx": (c + by) % n}, device_id_type=MESH)
    pl.semaphore_signal(barrier, inc=1, device_id={"sub": 1 - s}, device_id_type=MESH)
    for by in range(1, nm):
        pl.semaphore_signal(barrier, inc=1, device_id={"mdl": (m + by) % nm}, device_id_type=MESH)

    def gate_copy(j):
        at = pl.ds(pl.multiple_of(j * width, width), width)
        return (
            pltpu.make_async_copy(gate_hbm.at[:, at], gate_buf.at[j % depth], gate_sem.at[j % depth]),
            pltpu.make_async_copy(up_hbm.at[:, at], up_buf.at[j % depth], up_sem.at[j % depth]),
        )

    def down_copy(j):
        at = pl.ds(pl.multiple_of(j * width, width), width)
        return pltpu.make_async_copy(down_hbm.at[at, :], down_buf.at[j % depth], down_sem.at[j % depth])

    def remote(src, dst, send, recv, to):
        return pltpu.make_async_remote_copy(
            src_ref=src, dst_ref=dst, send_sem=send, recv_sem=recv, device_id={"ctx": to}, device_id_type=MESH
        )

    lower = (c + n - 1) % n
    upper = (c + 1) % n
    lo_rows, hi_rows = pl.ds(0, half), pl.ds(half, half)

    def lo_first(j):
        return remote(own.at[j, lo_rows], sum_lo.at[j], lo_send.at[j], lo_recv.at[j], lower)

    def lo_next(j):
        return remote(sum_lo.at[j], sum_lo.at[j], lo_send.at[j], lo_recv.at[j], lower)

    def hi_first(j):
        return remote(own.at[j, hi_rows], sum_hi.at[j], hi_send.at[j], hi_recv.at[j], upper)

    def hi_next(j):
        return remote(sum_hi.at[j], sum_hi.at[j], hi_send.at[j], hi_recv.at[j], upper)

    def hid_lo(j):
        return remote(hid.at[j, lo_rows], hid.at[j, lo_rows], hlo_send.at[j], hlo_recv.at[j], upper)

    def hid_hi(j):
        return remote(hid.at[j, hi_rows], hid.at[j, hi_rows], hhi_send.at[j], hhi_recv.at[j], lower)

    for j in range(min(depth - 1, chunks)):
        for copy in gate_copy(j):
            copy.start()
        down_copy(j).start()
    acc[...] = jnp.zeros_like(acc)
    pl.semaphore_wait(barrier, 2 + 1 + nm - 1)

    def valid(j):
        return jnp.logical_and(j >= 0, j < chunks)

    def activated(total):
        gate, up = total[:, :width], total[:, width:]
        return (gate / (1.0 + jnp.exp(-gate)) * up).astype(jnp.bfloat16)

    def step(t, carry):
        @pl.when(t < chunks)
        def _():
            for copy in gate_copy(t):
                copy.wait()

            @pl.when(t + depth - 1 < chunks)
            def _():
                for copy in gate_copy(t + depth - 1):
                    copy.start()

            x = x_ref[...]
            own[t, :, :width] = jnp.dot(
                x, gate_buf[t % depth], preferred_element_type=jnp.float32
            ).astype(jnp.bfloat16)
            own[t, :, width:] = jnp.dot(
                x, up_buf[t % depth], preferred_element_type=jnp.float32
            ).astype(jnp.bfloat16)

        a = t - lag * (n - 1 - c)

        @pl.when(jnp.logical_and(valid(a), c == n - 1))
        def _():
            lo_first(a).start()

        @pl.when(jnp.logical_and(valid(a), c < n - 1))
        def _():
            lo_next(a).wait_recv()
            total = sum_lo[a].astype(jnp.float32) + own[a, :half].astype(jnp.float32)

            @pl.when(c > 0)
            def _():
                sum_lo[a] = total.astype(jnp.bfloat16)
                lo_next(a).start()

            @pl.when(c == 0)
            def _():
                hid[a, :half] = activated(total)
                hid_lo(a).start()

        b = t - lag * c

        @pl.when(jnp.logical_and(valid(b), c == 0))
        def _():
            hi_first(b).start()

        @pl.when(jnp.logical_and(valid(b), c > 0))
        def _():
            hi_next(b).wait_recv()
            total = sum_hi[b].astype(jnp.float32) + own[b, half:].astype(jnp.float32)

            @pl.when(c < n - 1)
            def _():
                sum_hi[b] = total.astype(jnp.bfloat16)
                hi_next(b).start()

            @pl.when(c == n - 1)
            def _():
                hid[b, half:] = activated(total)
                hid_hi(b).start()

        ha = t - lag * (n - 1) - lag * c

        @pl.when(jnp.logical_and(valid(ha), c > 0))
        def _():
            hid_lo(ha).wait_recv()

            @pl.when(c < n - 1)
            def _():
                hid_lo(ha).start()

        hb = t - lag * (n - 1) - lag * (n - 1 - c)

        @pl.when(jnp.logical_and(valid(hb), c < n - 1))
        def _():
            hid_hi(hb).wait_recv()

            @pl.when(c > 0)
            def _():
                hid_hi(hb).start()

        d = t - 2 * lag * (n - 1)

        @pl.when(valid(d))
        def _():
            down_copy(d).wait()

            @pl.when(d + depth - 1 < chunks)
            def _():
                down_copy(d + depth - 1).start()

            acc[...] += jnp.dot(hid[d], down_buf[d % depth], preferred_element_type=jnp.float32)

        return carry

    lax.fori_loop(0, chunks + 2 * lag * (n - 1), step, 0)

    sum_over_heads(nm, m, s, acc, pair_out, pair_in, cross_out, cross_in,
                   pair_send, pair_recv, cross_send, cross_recv, out_ref)

    def drain(j, carry):
        @pl.when(c == n - 1)
        def _():
            lo_first(j).wait_send()

        @pl.when(jnp.logical_and(c > 0, c < n - 1))
        def _():
            lo_next(j).wait_send()
            hi_next(j).wait_send()

        @pl.when(c == 0)
        def _():
            hi_first(j).wait_send()

        @pl.when(c < n - 1)
        def _():
            hid_lo(j).wait_send()

        @pl.when(c > 0)
        def _():
            hid_hi(j).wait_send()

        return carry

    lax.fori_loop(0, chunks, drain, 0)


def sum_over_heads(nm, m, s, acc, pair_out, pair_in, cross_out, cross_in,
                   pair_send, pair_recv, cross_send, cross_recv, out_ref):
    share = out_ref.shape[0]
    for k in range(nm):
        at = pl.multiple_of((2 * k + 1 - s) * share, share)
        pair_out[k] = acc[pl.ds(at, share), :].astype(jnp.bfloat16)
    pair = pltpu.make_async_remote_copy(
        src_ref=pair_out, dst_ref=pair_in, send_sem=pair_send, recv_sem=pair_recv,
        device_id={"sub": 1 - s}, device_id_type=MESH,
    )
    pair.start()
    pair.wait_recv()
    crossing = []
    for by in range(1, nm):
        to = (m + by) % nm
        at = pl.multiple_of((2 * to + s) * share, share)
        cross_out[by - 1] = (acc[pl.ds(at, share), :] + pair_in[to].astype(jnp.float32)).astype(jnp.bfloat16)
        copy = pltpu.make_async_remote_copy(
            src_ref=cross_out.at[by - 1], dst_ref=cross_in.at[by - 1],
            send_sem=cross_send.at[by - 1], recv_sem=cross_recv.at[by - 1],
            device_id={"mdl": to}, device_id_type=MESH,
        )
        copy.start()
        crossing.append(copy)
    at = pl.multiple_of((2 * m + s) * share, share)
    total = acc[pl.ds(at, share), :] + pair_in[m].astype(jnp.float32)
    for by in range(1, nm):
        crossing[by - 1].wait_recv()
        total += cross_in[by - 1].astype(jnp.float32)
    out_ref[...] = total
    pair.wait_send()
    for copy in crossing:
        copy.wait_send()


def feed_forward(all_rows, gate_weight, up_weight, down_weight):
    n, nm = lax.axis_size("ctx"), lax.axis_size("mdl")
    rows, depth_in = all_rows.shape
    units = gate_weight.shape[1]
    columns = down_weight.shape[1]
    width = 256
    chunks = units // width
    share = rows // (2 * nm)
    bf, f32 = jnp.bfloat16, jnp.float32
    bufs = 3
    dma = pltpu.SemaphoreType.DMA
    return pl.pallas_call(
        functools.partial(ffn_kernel, n, nm, LAG),
        out_shape=jax.ShapeDtypeStruct((share, columns), f32),
        in_specs=[pl.BlockSpec(memory_space=pltpu.VMEM)] + [pl.BlockSpec(memory_space=pl.ANY)] * 3,
        out_specs=pl.BlockSpec(memory_space=pltpu.VMEM),
        scratch_shapes=[
            pltpu.VMEM((chunks, rows, 2 * width), bf),
            pltpu.VMEM((chunks, rows // 2, 2 * width), bf),
            pltpu.VMEM((chunks, rows // 2, 2 * width), bf),
            pltpu.VMEM((chunks, rows, width), bf),
            pltpu.VMEM((bufs, depth_in, width), bf),
            pltpu.VMEM((bufs, depth_in, width), bf),
            pltpu.VMEM((bufs, width, columns), bf),
            pltpu.VMEM((rows, columns), f32),
            pltpu.VMEM((nm, share, columns), bf),
            pltpu.VMEM((nm, share, columns), bf),
            pltpu.VMEM((nm - 1, share, columns), bf),
            pltpu.VMEM((nm - 1, share, columns), bf),
            dma((bufs,)), dma((bufs,)), dma((bufs,)),
        ] + [dma((chunks,))] * 8 + [dma, dma, dma((nm - 1,)), dma((nm - 1,))],
        compiler_params=pltpu.CompilerParams(
            collective_id=1, has_side_effects=True, vmem_limit_bytes=52 << 20
        ),
        name="feed_forward",
    )(all_rows, gate_weight, up_weight, down_weight)


HEADS = 2
NOT_VISIBLE = -1e30


def attend_kernel(
    n, nm, lag, score_scale, per_group,
    q_ref, kv_ref, bias_ref, residual_ref, out_hbm, hidden_ref, rows_ref,
    q_all, value_t, scores, own, own_stat, sum_lo, sum_hi, stat_lo, stat_hi, attn, out_buf,
    acc, pair_out, pair_in, cross_out, cross_in, projected, squares, gathered,
    out_sem, q_send, q_recv,
    lo_send, lo_recv, hi_send, hi_recv, slo_send, slo_recv, shi_send, shi_recv,
    alo_send, alo_recv, ahi_send, ahi_recv,
    pair_send, pair_recv, cross_send, cross_recv, square_send, square_recv,
    near_send, near_recv, far_send, far_recv,
):
    c = lax.axis_index("ctx")
    m = lax.axis_index("mdl")
    s = lax.axis_index("sub")
    chunks, rows, width = q_all.shape
    half = rows // 2
    block = q_ref.shape[0]
    slots = kv_ref.shape[1]
    head_dim = width // HEADS
    f32, bf = jnp.float32, jnp.bfloat16

    barrier = pltpu.get_barrier_semaphore()
    for by in range(1, n):
        pl.semaphore_signal(barrier, inc=1, device_id={"ctx": (c + by) % n}, device_id_type=MESH)
    pl.semaphore_signal(barrier, inc=1, device_id={"sub": 1 - s}, device_id_type=MESH)
    for by in range(1, nm):
        pl.semaphore_signal(barrier, inc=1, device_id={"mdl": (m + by) % nm}, device_id_type=MESH)

    def out_copy(j):
        at = pl.ds(pl.multiple_of(j * width, width), width)
        return pltpu.make_async_copy(out_hbm.at[at, :], out_buf.at[j], out_sem.at[j])

    def remote(src, dst, send, recv, to):
        return pltpu.make_async_remote_copy(
            src_ref=src, dst_ref=dst, send_sem=send, recv_sem=recv, device_id={"ctx": to}, device_id_type=MESH
        )

    def block_at(index):
        return pl.ds(pl.multiple_of(index * block, block), block)

    def query_copy(j, by):
        return remote(
            q_ref.at[:, pl.ds(j * width, width)], q_all.at[j, block_at(c), :],
            q_send.at[j, by - 1], q_recv.at[j, c], (c + by) % n,
        )

    def query_arrival(j, source):
        piece = q_all.at[j, block_at(source), :]
        return remote(piece, piece, q_send.at[j, 0], q_recv.at[j, source], source)

    for j in range(chunks):
        out_copy(j).start()
    acc[...] = jnp.zeros_like(acc)
    pl.semaphore_wait(barrier, n - 1 + 1 + nm - 1)

    for j in range(chunks):
        for by in range(1, n):
            query_copy(j, by).start()
    for j in range(chunks):
        q_all[j, block_at(c), :] = q_ref[:, j * width:(j + 1) * width]
    for g in range(kv_ref.shape[0]):
        for at in range(0, slots, 512):
            value_t[g, :, at:at + 512] = kv_ref[g, at:at + 512, head_dim:].T

    lower = (c + n - 1) % n
    upper = (c + 1) % n
    lo_rows, hi_rows = pl.ds(0, half), pl.ds(half, half)

    def lo_copies(j, first):
        return (
            remote(own.at[j, 0] if first else sum_lo.at[j], sum_lo.at[j], lo_send.at[j], lo_recv.at[j], lower),
            remote(own_stat.at[j, 0] if first else stat_lo.at[j], stat_lo.at[j], slo_send.at[j], slo_recv.at[j], lower),
        )

    def hi_copies(j, first):
        return (
            remote(own.at[j, 1] if first else sum_hi.at[j], sum_hi.at[j], hi_send.at[j], hi_recv.at[j], upper),
            remote(own_stat.at[j, 1] if first else stat_hi.at[j], stat_hi.at[j], shi_send.at[j], shi_recv.at[j], upper),
        )

    def attn_lo(j):
        return remote(attn.at[j, lo_rows], attn.at[j, lo_rows], alo_send.at[j], alo_recv.at[j], upper)

    def attn_hi(j):
        return remote(attn.at[j, hi_rows], attn.at[j, hi_rows], ahi_send.at[j], ahi_recv.at[j], lower)

    def valid(j):
        return jnp.logical_and(j >= 0, j < chunks)

    def merged(j, side, came, came_stat):
        result = []
        for h in range(HEADS):
            at = slice(h * head_dim, (h + 1) * head_dim)
            max_a, max_b = came_stat[j, h:h + 1, :], own_stat[j, side, h:h + 1, :]
            sum_a = came_stat[j, HEADS + h:HEADS + h + 1, :]
            sum_b = own_stat[j, side, HEADS + h:HEADS + h + 1, :]
            top = jnp.maximum(max_a, max_b)
            weight_a, weight_b = jnp.exp2(max_a - top), jnp.exp2(max_b - top)
            result.append((
                top,
                weight_a * sum_a + weight_b * sum_b,
                weight_a * came[j, at, :].astype(f32) + weight_b * own[j, side, at, :].astype(f32),
            ))
        return result

    def put(j, state, to, to_stat):
        for h, (top, total, weighted) in enumerate(state):
            to[j, h * head_dim:(h + 1) * head_dim, :] = weighted.astype(bf)
            to_stat[j, h:h + 1, :] = top
            to_stat[j, HEADS + h:HEADS + h + 1, :] = total

    def finish(j, state, first_row):
        for h, (_, total, weighted) in enumerate(state):
            attn[j, first_row:first_row + half, h * head_dim:(h + 1) * head_dim] = (weighted / total).T.astype(bf)

    span = 512

    def attend(j):
        group = j * HEADS // per_group
        spans = range(0, slots, span)

        def score(h, at, top):
            part = lax.dot_general(
                kv_ref[group, at:at + span, :head_dim], q_all[j, :, h * head_dim:(h + 1) * head_dim],
                (((1,), (1,)), ((), ())), preferred_element_type=f32,
            ) * score_scale + bias_ref[at:at + span, :]
            scores[h, at:at + span, :] = part
            return jnp.maximum(top, jnp.max(part, axis=0, keepdims=True))

        def weigh(h, at, top, total, weighted):
            prob = jnp.exp2(scores[h, at:at + span, :] - top)
            total += jnp.sum(prob, axis=0, keepdims=True)
            weighted += jnp.dot(value_t[group, :, at:at + span], prob.astype(bf), preferred_element_type=f32)
            return total, weighted

        lowest = jnp.full((1, rows), NOT_VISIBLE, f32)
        top = lowest
        for at in spans:
            top = score(0, at, top)
        for h in range(HEADS):
            next_top = lowest
            total, weighted = jnp.zeros((1, rows), f32), jnp.zeros((head_dim, rows), f32)
            for at in spans:
                if h + 1 < HEADS:
                    next_top = score(h + 1, at, next_top)
                total, weighted = weigh(h, at, top, total, weighted)
            for side in range(2):
                lanes = slice(side * half, (side + 1) * half)
                own[j, side, h * head_dim:(h + 1) * head_dim, :] = weighted[:, lanes].astype(bf)
                own_stat[j, side, h:h + 1, :] = top[:, lanes]
                own_stat[j, side, HEADS + h:HEADS + h + 1, :] = total[:, lanes]
            top = next_top

    own_stat[...] = jnp.zeros_like(own_stat)

    def step(t, carry):
        @pl.when(t < chunks)
        def _():
            for by in range(1, n):
                query_arrival(t, (c + by) % n).wait_recv()
            attend(t)

        a = t - lag * (n - 1 - c)

        @pl.when(jnp.logical_and(valid(a), c == n - 1))
        def _():
            for copy in lo_copies(a, True):
                copy.start()

        @pl.when(jnp.logical_and(valid(a), c < n - 1))
        def _():
            for copy in lo_copies(a, False):
                copy.wait_recv()
            state = merged(a, 0, sum_lo, stat_lo)

            @pl.when(c > 0)
            def _():
                put(a, state, sum_lo, stat_lo)
                for copy in lo_copies(a, False):
                    copy.start()

            @pl.when(c == 0)
            def _():
                finish(a, state, 0)
                attn_lo(a).start()

        b = t - lag * c

        @pl.when(jnp.logical_and(valid(b), c == 0))
        def _():
            for copy in hi_copies(b, True):
                copy.start()

        @pl.when(jnp.logical_and(valid(b), c > 0))
        def _():
            for copy in hi_copies(b, False):
                copy.wait_recv()
            state = merged(b, 1, sum_hi, stat_hi)

            @pl.when(c < n - 1)
            def _():
                put(b, state, sum_hi, stat_hi)
                for copy in hi_copies(b, False):
                    copy.start()

            @pl.when(c == n - 1)
            def _():
                finish(b, state, half)
                attn_hi(b).start()

        ha = t - lag * (n - 1) - lag * c

        @pl.when(jnp.logical_and(valid(ha), c > 0))
        def _():
            attn_lo(ha).wait_recv()

            @pl.when(c < n - 1)
            def _():
                attn_lo(ha).start()

        hb = t - lag * (n - 1) - lag * (n - 1 - c)

        @pl.when(jnp.logical_and(valid(hb), c < n - 1))
        def _():
            attn_hi(hb).wait_recv()

            @pl.when(c > 0)
            def _():
                attn_hi(hb).start()

        d = t - 2 * lag * (n - 1)

        @pl.when(valid(d))
        def _():
            out_copy(d).wait()
            acc[...] += jnp.dot(attn[d], out_buf[d], preferred_element_type=f32)

        return carry

    lax.fori_loop(0, chunks + 2 * lag * (n - 1), step, 0)

    sum_over_heads(nm, m, s, acc, pair_out, pair_in, cross_out, cross_in,
                   pair_send, pair_recv, cross_send, cross_recv, projected)

    share = hidden_ref.shape[0]
    hidden = residual_ref[...].astype(f32) + projected[...]
    hidden_ref[...] = hidden
    squares[c] = jnp.broadcast_to(jnp.sum(hidden * hidden, axis=1, keepdims=True), squares.shape[1:])
    for by in range(1, n):
        remote(squares.at[c], squares.at[c], square_send.at[by - 1], square_recv.at[c], (c + by) % n).start()
    for by in range(1, n):
        source = (c + by) % n
        remote(squares.at[source], squares.at[source], square_send.at[by - 1], square_recv.at[source], source).wait_recv()
    square_sum = jnp.sum(squares[...], axis=0)[:, :1]
    mine = 2 * m + s
    gathered[mine] = (hidden_ref[...] * lax.rsqrt(square_sum / D + 1e-05)).astype(bf)

    def to_mdl(index, by, recv, to):
        return pltpu.make_async_remote_copy(
            src_ref=gathered.at[index], dst_ref=gathered.at[index], send_sem=far_send.at[by - 1],
            recv_sem=recv, device_id={"mdl": to}, device_id_type=MESH,
        )

    def to_sub(k, index):
        return pltpu.make_async_remote_copy(
            src_ref=gathered.at[index], dst_ref=gathered.at[index], send_sem=near_send.at[k],
            recv_sem=near_recv.at[k], device_id={"sub": 1 - s}, device_id_type=MESH,
        )

    for by in range(1, nm):
        to_mdl(mine, by, far_recv.at[m], (m + by) % nm).start()
    to_sub(m, mine).start()
    for by in range(1, nm):
        k = (m + by) % nm
        to_mdl(2 * k + s, by, far_recv.at[k], k).wait_recv()
        to_sub(k, 2 * k + s).start()
    for k in range(nm):
        to_sub(k, 2 * k + 1 - s).wait_recv()
    for index in range(2 * nm):
        rows_ref[index * share:(index + 1) * share, :] = gathered[index]

    for by in range(1, nm):
        to_mdl(mine, by, far_recv.at[m], (m + by) % nm).wait_send()
    for k in range(nm):
        to_sub(k, 2 * k + s).wait_send()
    for by in range(1, n):
        remote(squares.at[c], squares.at[c], square_send.at[by - 1], square_recv.at[c], (c + by) % n).wait_send()
    for j in range(chunks):
        for by in range(1, n):
            query_copy(j, by).wait_send()

    def drain(j, carry):
        @pl.when(c == n - 1)
        def _():
            for copy in lo_copies(j, True):
                copy.wait_send()

        @pl.when(jnp.logical_and(c > 0, c < n - 1))
        def _():
            for copy in lo_copies(j, False) + hi_copies(j, False):
                copy.wait_send()

        @pl.when(c == 0)
        def _():
            for copy in hi_copies(j, True):
                copy.wait_send()

        @pl.when(c < n - 1)
        def _():
            attn_lo(j).wait_send()

        @pl.when(c > 0)
        def _():
            attn_hi(j).wait_send()

        return carry

    lax.fori_loop(0, chunks, drain, 0)


def attend_and_project(queries, cache_slots, bias, residual, out_weight):
    n, nm = lax.axis_size("ctx"), lax.axis_size("mdl")
    block, heads_width = queries.shape
    slots, group_heads, both = cache_slots.shape
    head_dim = both // 2
    width = HEADS * head_dim
    chunks = heads_width // width
    per_group = heads_width // head_dim // group_heads
    rows = block * n
    half = rows // 2
    share, columns = residual.shape
    bf, f32 = jnp.bfloat16, jnp.float32
    dma = pltpu.SemaphoreType.DMA
    vmem = pl.BlockSpec(memory_space=pltpu.VMEM)
    return pl.pallas_call(
        functools.partial(attend_kernel, n, nm, LAG, head_dim ** (-0.5) * LOG2_E, per_group),
        out_shape=(
            jax.ShapeDtypeStruct((share, columns), f32),
            jax.ShapeDtypeStruct((rows, columns), bf),
        ),
        in_specs=[vmem] * 4 + [pl.BlockSpec(memory_space=pl.ANY)],
        out_specs=(vmem, vmem),
        scratch_shapes=[
            pltpu.VMEM((chunks, rows, width), bf),
            pltpu.VMEM((group_heads, head_dim, slots), bf),
            pltpu.VMEM((HEADS, slots, rows), f32),
            pltpu.VMEM((chunks, 2, width, half), bf),
            pltpu.VMEM((chunks, 2, 8, half), f32),
            pltpu.VMEM((chunks, width, half), bf),
            pltpu.VMEM((chunks, width, half), bf),
            pltpu.VMEM((chunks, 8, half), f32),
            pltpu.VMEM((chunks, 8, half), f32),
            pltpu.VMEM((chunks, rows, width), bf),
            pltpu.VMEM((chunks, width, columns), bf),
            pltpu.VMEM((rows, columns), f32),
            pltpu.VMEM((nm, share, columns), bf),
            pltpu.VMEM((nm, share, columns), bf),
            pltpu.VMEM((nm - 1, share, columns), bf),
            pltpu.VMEM((nm - 1, share, columns), bf),
            pltpu.VMEM((share, columns), f32),
            pltpu.VMEM((n, share, 128), f32),
            pltpu.VMEM((2 * nm, share, columns), bf),
            dma((chunks,)), dma((chunks, n - 1)), dma((chunks, n)),
        ] + [dma((chunks,))] * 12 + [
            dma, dma, dma((nm - 1,)), dma((nm - 1,)), dma((n - 1,)), dma((n,)),
            dma((nm,)), dma((nm,)), dma((nm - 1,)), dma((nm,)),
        ],
        compiler_params=pltpu.CompilerParams(
            collective_id=2, has_side_effects=True, vmem_limit_bytes=52 << 20
        ),
        name="attend",
    )(queries, jnp.transpose(cache_slots, (1, 0, 2)), bias, residual, out_weight)


PARTS = 2
HOP1 = 2
HOP2 = 2
RING = 7 * HOP2 + 4
QUERY_GROUPS = 2
STAT_ROWS = 16
SEND_AT = (1, 3)
PASS_AT = (5, 8)


def block_kernel(
    n, nm, score_scale, per_group, width_total,
    position_ref, fill_ref, end_ref, q_ref, kv_ref, residual_ref, out_hbm, gate_hbm, up_hbm, down_hbm,
    hidden_ref, out_ref,
    bias, q_all, value_t, scores, tops, own_a, in_a, mid_a, attn, out_buf, acc_a,
    x_all, square, scale,
    own, sum_lo, sum_hi, hid, gate_buf, up_buf, down_buf, acc,
    pair_out, pair_in, cross_out, cross_in,
    out_sem, q_send, q_recv, q_pass, in_send, in_recv, mid_send, mid_recv,
    ax_send, ax_recv, near_a_send, near_a_recv, far_a_send, far_a_recv,
    pair_send, pair_recv, cross_send, cross_recv, square_send, square_recv,
    gx_send, gx_recv, gs_send, gs_recv,
    gate_sem, up_sem, down_sem,
    lo_send, lo_recv, hi_send, hi_recv, hlo_send, hlo_recv, hhi_send, hhi_recv,
):
    c = lax.axis_index("ctx")
    m = lax.axis_index("mdl")
    s = lax.axis_index("sub")
    f32, bf = jnp.float32, jnp.bfloat16
    items, _, rows, head_dim = attn.shape
    pair_width = HEADS * head_dim
    heads = items // PARTS
    group_heads = heads // QUERY_GROUPS
    group_width = group_heads * pair_width
    slots = kv_ref.shape[1]
    piece = rows // n
    share = rows // (2 * nm)
    mine = 2 * m + s

    barrier = pltpu.get_barrier_semaphore()
    for by in range(1, n):
        pl.semaphore_signal(barrier, inc=1, device_id={"ctx": (c + by) % n}, device_id_type=MESH)
    pl.semaphore_signal(barrier, inc=1, device_id={"sub": 1 - s}, device_id_type=MESH)
    for by in range(1, nm):
        pl.semaphore_signal(barrier, inc=1, device_id={"mdl": (m + by) % nm}, device_id_type=MESH)

    def remote(src, dst, send, recv, to, axis="ctx"):
        return pltpu.make_async_remote_copy(
            src_ref=src, dst_ref=dst, send_sem=send, recv_sem=recv, device_id={axis: to}, device_id_type=MESH
        )

    def out_copy(j):
        at = pl.ds(pl.multiple_of(j * pair_width, pair_width), pair_width)
        return pltpu.make_async_copy(out_hbm.at[at, :], out_buf.at[j], out_sem.at[j])

    width = hid.shape[2]
    chunks = gate_hbm.shape[1] // width
    units = PARTS * chunks
    depth = gate_buf.shape[0]

    def gate_copy(i):
        at = pl.ds(pl.multiple_of((i % chunks) * width, width), width)
        return (
            pltpu.make_async_copy(gate_hbm.at[:, at], gate_buf.at[i % depth], gate_sem.at[i % depth]),
            pltpu.make_async_copy(up_hbm.at[:, at], up_buf.at[i % depth], up_sem.at[i % depth]),
        )

    def down_copy(i):
        at = pl.ds(pl.multiple_of((i % chunks) * width, width), width)
        return pltpu.make_async_copy(down_hbm.at[at, :], down_buf.at[i % depth], down_sem.at[i % depth])

    def piece_at(index):
        return pl.ds(pl.multiple_of(index * piece, piece), piece)

    left = c < n // 2
    inner = jnp.where(left, c + 1, c - 1)
    outer = jnp.where(left, jnp.maximum(c - 1, 0), jnp.minimum(c + 1, n - 1))
    end = jnp.logical_or(c == 0, c == n - 1)
    middle = jnp.logical_not(end)
    keep = jnp.where(left, 0, 1)
    give = 1 - keep
    far = n - 1 - outer

    def query_copy(p, k, by):
        return remote(
            q_ref.at[p * piece:(p + 1) * piece, k * group_width:(k + 1) * group_width], q_all.at[p, k, piece_at(c), :],
            q_send.at[p, k, by - 1], q_recv.at[p, k, c], (c + by) % n,
        )

    def direct(by):
        return jnp.logical_or(middle, (c + by) % n != n - 1 - c)

    def send_queries(p, k):
        for by in (2, 1, 3):
            pl.when(direct(by))(query_copy(p, k, by).start)

    def drain_queries(p, k):
        for by in range(1, n):
            pl.when(direct(by))(query_copy(p, k, by).wait_send)
        pl.when(middle)(query_pass(p, k).wait_send)

    def query_arrival(p, k, source):
        there = q_all.at[p, k, piece_at(source), :]
        return remote(there, there, q_send.at[p, k, 0], q_recv.at[p, k, source], source)

    def query_pass(p, k):
        there = q_all.at[p, k, piece_at(far), :]
        return remote(there, there, q_pass.at[p, k], q_recv.at[p, k, far], outer)

    def pass_queries(p, k):
        @pl.when(middle)
        def _():
            query_arrival(p, k, far).wait_recv()
            query_pass(p, k).start()

    def wait_queries(p, k):
        for by in range(1, n):
            source = (c + by) % n
            pl.when(jnp.logical_or(end, source != far))(query_arrival(p, k, source).wait_recv)

    pl.semaphore_wait(barrier, n - 1 + 1 + nm - 1)
    for k in range(QUERY_GROUPS):
        send_queries(0, k)
    for j in range(heads):
        out_copy(j).start()
    for p in range(PARTS):
        for k in range(QUERY_GROUPS):
            q_all[p, k, piece_at(c), :] = q_ref[p * piece:(p + 1) * piece, k * group_width:(k + 1) * group_width]
    for i in range(depth - 1):
        for copy in gate_copy(i):
            copy.start()
        down_copy(i).start()

    fill = fill_ref[0]
    row = lax.broadcasted_iota(jnp.int32, (1, rows), 1)
    image = ((row // share) * (PARTS * share) + row % share) // IMG_TOK
    limits = jnp.zeros((1, rows), jnp.int32)
    for k in range(IMAGES):
        limits = jnp.where(image == k, end_ref[k], limits)
    lane = lax.broadcasted_iota(jnp.int32, (1, 128), 1)
    for k in range(slots // 128):
        tags = jnp.where(lane + k * 128 < fill, position_ref[k:k + 1, :], 2**30).astype(f32)
        column = jnp.broadcast_to(tags, (128, 128)).T[:, :1]
        bias[k * 128:(k + 1) * 128, :] = jnp.where(column <= limits.astype(f32), 0.0, NOT_VISIBLE)
    for g in range(kv_ref.shape[0]):
        for at in range(0, slots, 512):
            value_t[g, :, at:at + 512] = kv_ref[g, at:at + 512, head_dim:].T
    acc_a[...] = jnp.zeros_like(acc_a)
    acc[...] = jnp.zeros_like(acc)

    def split(x, count):
        terms = []
        for _ in range(count):
            terms.append(x.astype(bf).astype(f32))
            x = x - terms[-1]
        return terms

    def put_partial(ref, at, top, total, weighted):
        ref[(*at, slice(0, head_dim), slice(None))] = weighted.astype(bf)
        terms = (*split(top, 3), *split(total, 2))
        line = lax.broadcasted_iota(jnp.int32, (STAT_ROWS, rows), 0)
        stat = jnp.zeros((STAT_ROWS, rows), f32)
        for k, term in enumerate(terms):
            stat = jnp.where(line == k, term, stat)
        ref[(*at, slice(head_dim, head_dim + STAT_ROWS), slice(None))] = stat.astype(bf)

    def merged(partials):
        stats = [x[head_dim:].astype(f32) for x in partials]
        tops_in = [stat[0:1] + stat[1:2] + stat[2:3] for stat in stats]
        top = functools.reduce(jnp.maximum, tops_in)
        total, weighted = 0.0, 0.0
        for x, stat, top_in in zip(partials, stats, tops_in):
            weight = jnp.exp2(top_in - top)
            total += weight * (stat[3:4] + stat[4:5])
            weighted += weight * x[:head_dim].astype(f32)
        return top, total, weighted

    span = 512
    spans = range(0, slots, span)
    both = HEADS * rows

    def group_of(i):
        return ((i % heads) * HEADS) // per_group

    def score(i, slot, at, top):
        j = i % heads
        base = (j % group_heads) * pair_width
        q = jnp.concatenate([
            q_all[i // heads, j // group_heads, :, pl.ds(pl.multiple_of(base + h * head_dim, head_dim), head_dim)]
            for h in range(HEADS)
        ], axis=0)
        part = lax.dot_general(
            kv_ref[group_of(i), at:at + span, :head_dim], q, (((1,), (1,)), ((), ())), preferred_element_type=f32,
        ) * score_scale + jnp.concatenate([bias[at:at + span, :]] * HEADS, axis=1)
        scores[slot, at:at + span, :] = part
        return jnp.maximum(top, jnp.max(part, axis=0, keepdims=True))

    def weigh(i, slot, at, top, total, weighted):
        prob = jnp.exp2(scores[slot, at:at + span, :] - top)
        total += jnp.sum(prob, axis=0, keepdims=True)
        weighted += jnp.dot(value_t[group_of(i), :, at:at + span], prob.astype(bf), preferred_element_type=f32)
        return total, weighted

    def attend(i, slot, more):
        top = tops[slot, 0:1, :]
        next_top = jnp.full((1, both), NOT_VISIBLE, f32)
        total, weighted = jnp.zeros((1, both), f32), jnp.zeros((head_dim, both), f32)
        for at in spans:
            if more:
                next_top = score(i + 1, 1 - slot, at, next_top)
            total, weighted = weigh(i, slot, at, top, total, weighted)
        if more:
            tops[1 - slot, 0:1, :] = next_top
        for h in range(HEADS):
            lanes = slice(h * rows, (h + 1) * rows)
            put_partial(own_a, (i, h), top[:, lanes], total[:, lanes], weighted[:, lanes])

    def inward(i):
        return remote(own_a.at[i], in_a.at[i], in_send.at[i], in_recv.at[i], inner)

    def across(i):
        return remote(in_a.at[i, give], mid_a.at[i], mid_send.at[i], mid_recv.at[i], inner)

    def attn_across(i, h):
        return remote(attn.at[i, h], attn.at[i, h], ax_send.at[i], ax_recv.at[i], inner)

    def attn_near(i, h, to):
        return remote(attn.at[i, h], attn.at[i, h], near_a_send.at[i], near_a_recv.at[i], to)

    def attn_far(i, h, to):
        return remote(attn.at[i, h], attn.at[i, h], far_a_send.at[i], far_a_recv.at[i], to)

    def valid(i, count):
        return jnp.logical_and(i >= 0, i < count)

    def pair_copy(e):
        return remote(pair_out.at[e], pair_in.at[e], pair_send.at[e], pair_recv.at[e], 1 - s, "sub")

    def cross_copy(e, by):
        return remote(
            cross_out.at[e, by - 1], cross_in.at[e, by - 1], cross_send.at[e, by - 1], cross_recv.at[e, by - 1],
            (m + by) % nm, "mdl",
        )

    def sum_pair(e, source, p):
        for k in range(nm):
            at = pl.multiple_of((2 * k + 1 - s) * share, share)
            pair_out[e, k] = source[p, pl.ds(at, share), :].astype(bf)
        pair_copy(e).start()

    def sum_cross(e, source, p):
        pair_copy(e).wait_recv()
        for by in range(1, nm):
            to = (m + by) % nm
            at = pl.multiple_of((2 * to + s) * share, share)
            cross_out[e, by - 1] = (source[p, pl.ds(at, share), :] + pair_in[e, to].astype(f32)).astype(bf)
            cross_copy(e, by).start()

    def sum_total(e, source, p):
        at = pl.multiple_of(mine * share, share)
        total = source[p, pl.ds(at, share), :] + pair_in[e, m].astype(f32)
        for by in range(1, nm):
            cross_copy(e, by).wait_recv()
            total += cross_in[e, by - 1].astype(f32)
        return total

    def sum_drain(e):
        pair_copy(e).wait_send()
        for by in range(1, nm):
            cross_copy(e, by).wait_send()

    def share_at(index):
        return pl.ds(pl.multiple_of(index * share, share), share)

    def to_mdl(p, index, by, recv, to):
        there = x_all.at[p, share_at(index), :]
        return remote(there, there, gx_send.at[p, by - 1], recv, to, "mdl")

    def to_sub(p, k, index):
        there = x_all.at[p, share_at(index), :]
        return remote(there, there, gs_send.at[p, k], gs_recv.at[p, k], 1 - s, "sub")

    def square_copy(p, by):
        return remote(square.at[p, c], square.at[p, c], square_send.at[p, by - 1], square_recv.at[p, c], (c + by) % n)

    def stream_rows(p):
        hidden = residual_ref[p * share:(p + 1) * share, :].astype(f32) + sum_total(p, acc_a, p)
        hidden_ref[p * share:(p + 1) * share, :] = hidden
        x_all[p, share_at(mine), :] = hidden.astype(bf)
        for by in range(1, nm):
            to_mdl(p, mine, by, gx_recv.at[p, m], (m + by) % nm).start()
        to_sub(p, m, mine).start()

    def stream_pass(p):
        for by in range(1, nm):
            k = (m + by) % nm
            to_mdl(p, 2 * k + s, by, gx_recv.at[p, k], k).wait_recv()
            to_sub(p, k, 2 * k + s).start()

    def stream_done(p):
        for k in range(nm):
            to_sub(p, k, 2 * k + 1 - s).wait_recv()
        x = x_all[p].astype(f32)
        total = jnp.sum(x * x, axis=1, keepdims=True)
        square[p, c] = jnp.broadcast_to(total, (rows, 128)).T[:8, :]
        for by in range(1, n):
            square_copy(p, by).start()

    def row_scale(p):
        for by in range(1, n):
            source = (c + by) % n
            remote(
                square.at[p, source], square.at[p, source], square_send.at[p, by - 1], square_recv.at[p, source], source
            ).wait_recv()
        mean = jnp.sum(square[p], axis=0)[:1, :] / width_total
        scale[p] = jnp.broadcast_to(lax.rsqrt(mean + 1e-05), (128, rows)).T

    def stream_drain(p):
        for by in range(1, nm):
            to_mdl(p, mine, by, gx_recv.at[p, m], (m + by) % nm).wait_send()
        for k in range(nm):
            to_sub(p, k, 2 * k + s).wait_send()
        for by in range(1, n):
            square_copy(p, by).wait_send()

    for k in range(QUERY_GROUPS):
        pass_queries(0, k)
    wait_queries(0, 0)
    top = jnp.full((1, both), NOT_VISIBLE, f32)
    for at in spans:
        top = score(0, 0, at, top)
    tops[0, 0:1, :] = top

    def drain_attention(i):
        pl.when(end)(inward(i).wait_send)

        @pl.when(middle)
        def _():
            across(i).wait_send()
            attn_across(i, keep).wait_send()
            attn_near(i, keep, outer).wait_send()
            attn_far(i, give, outer).wait_send()

    last = n * HOP1
    steps = items + last
    ready = heads - 1 + last

    def attention_step(t, slot):
        for k in range(QUERY_GROUPS):
            pl.when(t == SEND_AT[k])(functools.partial(send_queries, 1, k))
            pl.when(t == PASS_AT[k])(functools.partial(pass_queries, 1, k))
        for k in range(1, PARTS * QUERY_GROUPS):
            pl.when(t + 1 == k * group_heads)(functools.partial(wait_queries, k // QUERY_GROUPS, k % QUERY_GROUPS))

        @pl.when(t < items - 1)
        def _():
            attend(t, slot, True)

        @pl.when(t == items - 1)
        def _():
            attend(t, slot, False)

        @pl.when(jnp.logical_and(end, valid(t, items)))
        def _():
            inward(t).start()

        a = t - HOP1

        @pl.when(jnp.logical_and(middle, valid(a, items)))
        def _():
            inward(a).wait_recv()
            put_partial(in_a, (a, give), *merged([own_a[a, give], in_a[a, give]]))
            across(a).start()

        b = t - 2 * HOP1

        @pl.when(jnp.logical_and(middle, valid(b, items)))
        def _():
            across(b).wait_recv()
            _, total, weighted = merged([own_a[b, keep], in_a[b, keep], mid_a[b]])
            attn[b, keep] = (weighted / total).T.astype(bf)
            attn_across(b, keep).start()
            attn_near(b, keep, outer).start()

        g = t - 3 * HOP1

        @pl.when(jnp.logical_and(middle, valid(g, items)))
        def _():
            attn_across(g, give).wait_recv()
            attn_far(g, give, outer).start()

        d = t - last

        @pl.when(valid(d, items))
        def _():
            @pl.when(end)
            def _():
                attn_near(d, keep, inner).wait_recv()
                attn_far(d, give, inner).wait_recv()

            @pl.when(d < heads)
            def _():
                out_copy(d).wait()

            p = d // heads
            both_heads = jnp.concatenate([attn[d, h] for h in range(HEADS)], axis=1)
            acc_a[p] += jnp.dot(both_heads, out_buf[d % heads], preferred_element_type=f32)

        @pl.when(valid(d - 1, items))
        def _():
            drain_attention(d - 1)

        for k, stage in (
            (0, lambda: sum_pair(0, acc_a, 0)), (1, lambda: sum_cross(0, acc_a, 0)), (3, lambda: stream_rows(0)),
            (5, lambda: stream_pass(0)),
        ):
            pl.when(t == ready + k)(stage)

    def attention_steps(u, carry):
        attention_step(2 * u, 0)
        attention_step(2 * u + 1, 1)
        return carry

    lax.fori_loop(0, steps // 2, attention_steps, 0)
    sum_pair(1, acc_a, 1)
    stream_done(0)

    lower = (c + n - 1) % n
    upper = (c + 1) % n
    half = rows // 2
    lo_rows, hi_rows = pl.ds(0, half), pl.ds(half, half)

    def lo_first(i):
        r = i % RING
        return remote(own.at[r, lo_rows], sum_lo.at[r], lo_send.at[r], lo_recv.at[r], lower)

    def lo_next(i):
        r = i % RING
        return remote(sum_lo.at[r], sum_lo.at[r], lo_send.at[r], lo_recv.at[r], lower)

    def hi_first(i):
        r = i % RING
        return remote(own.at[r, hi_rows], sum_hi.at[r], hi_send.at[r], hi_recv.at[r], upper)

    def hi_next(i):
        r = i % RING
        return remote(sum_hi.at[r], sum_hi.at[r], hi_send.at[r], hi_recv.at[r], upper)

    def hid_lo(i):
        r = i % RING
        return remote(hid.at[r, lo_rows], hid.at[r, lo_rows], hlo_send.at[r], hlo_recv.at[r], upper)

    def hid_hi(i):
        r = i % RING
        return remote(hid.at[r, hi_rows], hid.at[r, hi_rows], hhi_send.at[r], hhi_recv.at[r], lower)

    def activated(total, i, first):
        by_row = scale[i // chunks, first:first + half, :1]
        gate, up = total[:, :width] * by_row, total[:, width:] * by_row
        return (gate / (1.0 + jnp.exp(-gate)) * up).astype(bf)

    def drain_units(i):
        @pl.when(c == n - 1)
        def _():
            lo_first(i).wait_send()

        @pl.when(jnp.logical_and(c > 0, c < n - 1))
        def _():
            lo_next(i).wait_send()
            hi_next(i).wait_send()

        @pl.when(c == 0)
        def _():
            hi_first(i).wait_send()

        @pl.when(c < n - 1)
        def _():
            hid_lo(i).wait_send()

        @pl.when(c > 0)
        def _():
            hid_hi(i).wait_send()

    turn = HOP2 * (n - 1)

    def unit_step(t, carry):
        for k, stage in enumerate((
            lambda: sum_cross(1, acc_a, 1), lambda: stream_rows(1), lambda: row_scale(0), lambda: stream_pass(1),
            lambda: stream_done(1), lambda: row_scale(1),
        )):
            pl.when(t == k + 1)(stage)

        @pl.when(t < units)
        def _():
            for copy in gate_copy(t):
                copy.wait()

            @pl.when(t + depth - 1 < units)
            def _():
                for copy in gate_copy(t + depth - 1):
                    copy.start()

            x = x_all[t // chunks]
            own[t % RING, :, :width] = jnp.dot(x, gate_buf[t % depth], preferred_element_type=f32).astype(bf)
            own[t % RING, :, width:] = jnp.dot(x, up_buf[t % depth], preferred_element_type=f32).astype(bf)

        a = t - HOP2 * (n - 1 - c)

        @pl.when(jnp.logical_and(valid(a, units), c == n - 1))
        def _():
            lo_first(a).start()

        @pl.when(jnp.logical_and(valid(a, units), c < n - 1))
        def _():
            lo_next(a).wait_recv()
            total = sum_lo[a % RING].astype(f32) + own[a % RING, :half].astype(f32)

            @pl.when(c > 0)
            def _():
                sum_lo[a % RING] = total.astype(bf)
                lo_next(a).start()

            @pl.when(c == 0)
            def _():
                hid[a % RING, :half] = activated(total, a, 0)
                hid_lo(a).start()

        b = t - HOP2 * c

        @pl.when(jnp.logical_and(valid(b, units), c == 0))
        def _():
            hi_first(b).start()

        @pl.when(jnp.logical_and(valid(b, units), c > 0))
        def _():
            hi_next(b).wait_recv()
            total = sum_hi[b % RING].astype(f32) + own[b % RING, half:].astype(f32)

            @pl.when(c < n - 1)
            def _():
                sum_hi[b % RING] = total.astype(bf)
                hi_next(b).start()

            @pl.when(c == n - 1)
            def _():
                hid[b % RING, half:] = activated(total, b, half)
                hid_hi(b).start()

        ha = t - turn - HOP2 * c

        @pl.when(jnp.logical_and(valid(ha, units), c > 0))
        def _():
            hid_lo(ha).wait_recv()

            @pl.when(c < n - 1)
            def _():
                hid_lo(ha).start()

        hb = t - turn - HOP2 * (n - 1 - c)

        @pl.when(jnp.logical_and(valid(hb, units), c < n - 1))
        def _():
            hid_hi(hb).wait_recv()

            @pl.when(c > 0)
            def _():
                hid_hi(hb).start()

        d = t - 2 * turn

        @pl.when(valid(d, units))
        def _():
            down_copy(d).wait()

            @pl.when(d + depth - 1 < units)
            def _():
                down_copy(d + depth - 1).start()

            acc[d // chunks] += jnp.dot(hid[d % RING], down_buf[d % depth], preferred_element_type=f32)

        @pl.when(valid(d - 1, units))
        def _():
            drain_units(d - 1)

        def first_out():
            out_ref[0:share, :] = sum_total(2, acc, 0)

        for k, stage in enumerate((lambda: sum_pair(2, acc, 0), lambda: sum_cross(2, acc, 0), first_out)):
            pl.when(d == chunks + 2 * k)(stage)

        return carry

    lax.fori_loop(0, units + 2 * turn, unit_step, 0)

    sum_pair(3, acc, 1)
    drain_attention(items - 1)
    drain_units(units - 1)
    for p in range(PARTS):
        for k in range(QUERY_GROUPS):
            drain_queries(p, k)
    for p in range(PARTS):
        stream_drain(p)
    for e in range(3):
        sum_drain(e)
    sum_cross(3, acc, 1)
    out_ref[share:2 * share, :] = sum_total(3, acc, 1)
    sum_drain(3)


def whole_block(
    queries, cache_slots, slot_position, shard_fill, image_end, residual, out_weight, gate_weight, up_weight, down_weight
):
    n, nm = lax.axis_size("ctx"), lax.axis_size("mdl")
    block, heads_width = queries.shape
    slots, group_heads, kv_width = cache_slots.shape
    head_dim = kv_width // 2
    pair_width = HEADS * head_dim
    heads = heads_width // pair_width
    items = PARTS * heads
    per_group = heads_width // head_dim // group_heads
    rows = block * n // PARTS
    half = rows // 2
    columns = residual.shape[1]
    share = rows // (2 * nm)
    width = 256
    bufs = 3
    bf, f32 = jnp.bfloat16, jnp.float32
    dma = pltpu.SemaphoreType.DMA
    vmem = pl.BlockSpec(memory_space=pltpu.VMEM)
    smem = pl.BlockSpec(memory_space=pltpu.SMEM)
    sums = 2 * PARTS
    return pl.pallas_call(
        functools.partial(block_kernel, n, nm, head_dim ** (-0.5) * LOG2_E, per_group, n * columns),
        out_shape=(
            jax.ShapeDtypeStruct((PARTS * share, columns), f32),
            jax.ShapeDtypeStruct((PARTS * share, columns), f32),
        ),
        in_specs=[vmem, smem, smem, vmem, vmem, vmem] + [pl.BlockSpec(memory_space=pl.ANY)] * 4,
        out_specs=(vmem, vmem),
        scratch_shapes=[
            pltpu.VMEM((slots, rows), f32),
            pltpu.VMEM((PARTS, QUERY_GROUPS, rows, heads_width // QUERY_GROUPS), bf),
            pltpu.VMEM((group_heads, head_dim, slots), bf),
            pltpu.VMEM((2, slots, HEADS * rows), f32),
            pltpu.VMEM((2, 8, HEADS * rows), f32),
            pltpu.VMEM((items, HEADS, head_dim + STAT_ROWS, rows), bf),
            pltpu.VMEM((items, HEADS, head_dim + STAT_ROWS, rows), bf),
            pltpu.VMEM((items, head_dim + STAT_ROWS, rows), bf),
            pltpu.VMEM((items, HEADS, rows, head_dim), bf),
            pltpu.VMEM((heads, pair_width, columns), bf),
            pltpu.VMEM((PARTS, rows, columns), f32),
            pltpu.VMEM((PARTS, rows, columns), bf),
            pltpu.VMEM((PARTS, n, 8, rows), f32),
            pltpu.VMEM((PARTS, rows, 128), f32),
            pltpu.VMEM((RING, rows, 2 * width), bf),
            pltpu.VMEM((RING, half, 2 * width), bf),
            pltpu.VMEM((RING, half, 2 * width), bf),
            pltpu.VMEM((RING, rows, width), bf),
            pltpu.VMEM((bufs, columns, width), bf),
            pltpu.VMEM((bufs, columns, width), bf),
            pltpu.VMEM((bufs, width, columns), bf),
            pltpu.VMEM((PARTS, rows, columns), f32),
            pltpu.VMEM((sums, nm, share, columns), bf),
            pltpu.VMEM((sums, nm, share, columns), bf),
            pltpu.VMEM((sums, nm - 1, share, columns), bf),
            pltpu.VMEM((sums, nm - 1, share, columns), bf),
            dma((heads,)), dma((PARTS, QUERY_GROUPS, n - 1)), dma((PARTS, QUERY_GROUPS, n)), dma((PARTS, QUERY_GROUPS)),
        ] + [dma((items,))] * 10 + [
            dma((sums,)), dma((sums,)), dma((sums, nm - 1)), dma((sums, nm - 1)), dma((PARTS, n - 1)), dma((PARTS, n)),
            dma((PARTS, nm - 1)), dma((PARTS, nm)), dma((PARTS, nm)), dma((PARTS, nm)),
            dma((bufs,)), dma((bufs,)), dma((bufs,)),
        ] + [dma((RING,))] * 8,
        compiler_params=pltpu.CompilerParams(
            collective_id=3, has_side_effects=True, vmem_limit_bytes=61 << 20
        ),
        name="block",
    )(
        slot_position.reshape(slots // 128, 128), shard_fill, image_end, queries,
        jnp.transpose(cache_slots, (1, 0, 2)), residual, out_weight, gate_weight, up_weight, down_weight,
    )


def fits_parts(queries, residual, n, nm):
    block, share = queries.shape[0], residual.shape[0]
    return n == 4 and block == share and block % (16 * PARTS) == 0 and IMG_TOK % block == 0 and block * n == PARTS * 128


def body(
    queries,
    cache_slots,
    slot_position,
    shard_fill,
    image_end,
    residual,
    out_weight,
    gate_weight,
    up_weight,
    down_weight,
):
    if fits_parts(queries, residual, lax.axis_size("ctx"), lax.axis_size("mdl")):
        return whole_block(
            queries, cache_slots, slot_position, shard_fill, image_end,
            residual, out_weight, gate_weight, up_weight, down_weight,
        )
    slot_index = jnp.arange(cache_slots.shape[0], dtype=jnp.int32)
    slot_tags = jnp.where(slot_index < shard_fill[0], slot_position, 2**30)
    limits = visible_limits(image_end, 0, queries.shape[0] * lax.axis_size("ctx"))
    bias = jnp.where(slot_tags[:, None] <= limits[None, :], 0.0, NOT_VISIBLE).astype(jnp.float32)
    hidden_state, all_rows = attend_and_project(queries, cache_slots, bias, residual, out_weight)
    forward_delta = feed_forward(all_rows, gate_weight, up_weight, down_weight)
    return (hidden_state, forward_delta)


def solution(mesh):
    in_specs = (
        P(("grp", "ctx"), ("mdl", "sub")),
        P(("grp", "ctx"), ("mdl", "sub"), None),
        P(("grp", "ctx")),
        P(("grp", "ctx")),
        P("grp"),
        P(("grp", "mdl", "sub"), "ctx"),
        P(("mdl", "sub"), "ctx"),
        P("ctx", ("mdl", "sub")),
        P("ctx", ("mdl", "sub")),
        P(("mdl", "sub"), "ctx"),
    )
    out_specs = (P(("grp", "mdl", "sub"), "ctx"), P(("grp", "mdl", "sub"), "ctx"))
    return jax.shard_map(body, mesh=mesh, in_specs=in_specs, out_specs=out_specs, check_vma=False)
```

```python
import functools

import jax
import jax.numpy as jnp
from jax import lax
from jax.experimental import pallas as pl
from jax.experimental.pallas import tpu as pltpu
from jax.sharding import PartitionSpec as P

D = 8192
IMAGES = 2
IMG_TOK = 128
LOG2_E = 1.4426950408889634


def visible_limits(image_end, first_row, query_count):
    row_index = first_row + jnp.arange(query_count, dtype=jnp.int32)
    image_index = row_index // IMG_TOK
    matches = image_index[:, None] == jnp.arange(IMAGES, dtype=jnp.int32)[None, :]
    return jnp.sum(jnp.where(matches, image_end[None, :], 0), axis=1)


MESH = pl.DeviceIdType.MESH
LAG = 3


def ffn_kernel(
    n, nm, lag, x_ref, gate_hbm, up_hbm, down_hbm, out_ref,
    own, sum_lo, sum_hi, hid, gate_buf, up_buf, down_buf, acc, pair_out, pair_in, cross_out, cross_in,
    gate_sem, up_sem, down_sem,
    lo_send, lo_recv, hi_send, hi_recv, hlo_send, hlo_recv, hhi_send, hhi_recv,
    pair_send, pair_recv, cross_send, cross_recv,
):
    c = lax.axis_index("ctx")
    m = lax.axis_index("mdl")
    s = lax.axis_index("sub")
    chunks = own.shape[0]
    rows = x_ref.shape[0]
    half = rows // 2
    width = hid.shape[2]
    depth = gate_buf.shape[0]

    barrier = pltpu.get_barrier_semaphore()
    for by in (1, n - 1):
        pl.semaphore_signal(barrier, inc=1, device_id={"ctx": (c + by) % n}, device_id_type=MESH)
    pl.semaphore_signal(barrier, inc=1, device_id={"sub": 1 - s}, device_id_type=MESH)
    for by in range(1, nm):
        pl.semaphore_signal(barrier, inc=1, device_id={"mdl": (m + by) % nm}, device_id_type=MESH)

    def gate_copy(j):
        at = pl.ds(pl.multiple_of(j * width, width), width)
        return (
            pltpu.make_async_copy(gate_hbm.at[:, at], gate_buf.at[j % depth], gate_sem.at[j % depth]),
            pltpu.make_async_copy(up_hbm.at[:, at], up_buf.at[j % depth], up_sem.at[j % depth]),
        )

    def down_copy(j):
        at = pl.ds(pl.multiple_of(j * width, width), width)
        return pltpu.make_async_copy(down_hbm.at[at, :], down_buf.at[j % depth], down_sem.at[j % depth])

    def remote(src, dst, send, recv, to):
        return pltpu.make_async_remote_copy(
            src_ref=src, dst_ref=dst, send_sem=send, recv_sem=recv, device_id={"ctx": to}, device_id_type=MESH
        )

    lower = (c + n - 1) % n
    upper = (c + 1) % n
    lo_rows, hi_rows = pl.ds(0, half), pl.ds(half, half)

    def lo_first(j):
        return remote(own.at[j, lo_rows], sum_lo.at[j], lo_send.at[j], lo_recv.at[j], lower)

    def lo_next(j):
        return remote(sum_lo.at[j], sum_lo.at[j], lo_send.at[j], lo_recv.at[j], lower)

    def hi_first(j):
        return remote(own.at[j, hi_rows], sum_hi.at[j], hi_send.at[j], hi_recv.at[j], upper)

    def hi_next(j):
        return remote(sum_hi.at[j], sum_hi.at[j], hi_send.at[j], hi_recv.at[j], upper)

    def hid_lo(j):
        return remote(hid.at[j, lo_rows], hid.at[j, lo_rows], hlo_send.at[j], hlo_recv.at[j], upper)

    def hid_hi(j):
        return remote(hid.at[j, hi_rows], hid.at[j, hi_rows], hhi_send.at[j], hhi_recv.at[j], lower)

    for j in range(min(depth - 1, chunks)):
        for copy in gate_copy(j):
            copy.start()
        down_copy(j).start()
    acc[...] = jnp.zeros_like(acc)
    pl.semaphore_wait(barrier, 2 + 1 + nm - 1)

    def valid(j):
        return jnp.logical_and(j >= 0, j < chunks)

    def activated(total):
        gate, up = total[:, :width], total[:, width:]
        return (gate / (1.0 + jnp.exp(-gate)) * up).astype(jnp.bfloat16)

    def step(t, carry):
        @pl.when(t < chunks)
        def _():
            for copy in gate_copy(t):
                copy.wait()

            @pl.when(t + depth - 1 < chunks)
            def _():
                for copy in gate_copy(t + depth - 1):
                    copy.start()

            x = x_ref[...]
            own[t, :, :width] = jnp.dot(
                x, gate_buf[t % depth], preferred_element_type=jnp.float32
            ).astype(jnp.bfloat16)
            own[t, :, width:] = jnp.dot(
                x, up_buf[t % depth], preferred_element_type=jnp.float32
            ).astype(jnp.bfloat16)

        a = t - lag * (n - 1 - c)

        @pl.when(jnp.logical_and(valid(a), c == n - 1))
        def _():
            lo_first(a).start()

        @pl.when(jnp.logical_and(valid(a), c < n - 1))
        def _():
            lo_next(a).wait_recv()
            total = sum_lo[a].astype(jnp.float32) + own[a, :half].astype(jnp.float32)

            @pl.when(c > 0)
            def _():
                sum_lo[a] = total.astype(jnp.bfloat16)
                lo_next(a).start()

            @pl.when(c == 0)
            def _():
                hid[a, :half] = activated(total)
                hid_lo(a).start()

        b = t - lag * c

        @pl.when(jnp.logical_and(valid(b), c == 0))
        def _():
            hi_first(b).start()

        @pl.when(jnp.logical_and(valid(b), c > 0))
        def _():
            hi_next(b).wait_recv()
            total = sum_hi[b].astype(jnp.float32) + own[b, half:].astype(jnp.float32)

            @pl.when(c < n - 1)
            def _():
                sum_hi[b] = total.astype(jnp.bfloat16)
                hi_next(b).start()

            @pl.when(c == n - 1)
            def _():
                hid[b, half:] = activated(total)
                hid_hi(b).start()

        ha = t - lag * (n - 1) - lag * c

        @pl.when(jnp.logical_and(valid(ha), c > 0))
        def _():
            hid_lo(ha).wait_recv()

            @pl.when(c < n - 1)
            def _():
                hid_lo(ha).start()

        hb = t - lag * (n - 1) - lag * (n - 1 - c)

        @pl.when(jnp.logical_and(valid(hb), c < n - 1))
        def _():
            hid_hi(hb).wait_recv()

            @pl.when(c > 0)
            def _():
                hid_hi(hb).start()

        d = t - 2 * lag * (n - 1)

        @pl.when(valid(d))
        def _():
            down_copy(d).wait()

            @pl.when(d + depth - 1 < chunks)
            def _():
                down_copy(d + depth - 1).start()

            acc[...] += jnp.dot(hid[d], down_buf[d % depth], preferred_element_type=jnp.float32)

        return carry

    lax.fori_loop(0, chunks + 2 * lag * (n - 1), step, 0)

    sum_over_heads(nm, m, s, acc, pair_out, pair_in, cross_out, cross_in,
                   pair_send, pair_recv, cross_send, cross_recv, out_ref)

    def drain(j, carry):
        @pl.when(c == n - 1)
        def _():
            lo_first(j).wait_send()

        @pl.when(jnp.logical_and(c > 0, c < n - 1))
        def _():
            lo_next(j).wait_send()
            hi_next(j).wait_send()

        @pl.when(c == 0)
        def _():
            hi_first(j).wait_send()

        @pl.when(c < n - 1)
        def _():
            hid_lo(j).wait_send()

        @pl.when(c > 0)
        def _():
            hid_hi(j).wait_send()

        return carry

    lax.fori_loop(0, chunks, drain, 0)


def sum_over_heads(nm, m, s, acc, pair_out, pair_in, cross_out, cross_in,
                   pair_send, pair_recv, cross_send, cross_recv, out_ref):
    share = out_ref.shape[0]
    for k in range(nm):
        at = pl.multiple_of((2 * k + 1 - s) * share, share)
        pair_out[k] = acc[pl.ds(at, share), :].astype(jnp.bfloat16)
    pair = pltpu.make_async_remote_copy(
        src_ref=pair_out, dst_ref=pair_in, send_sem=pair_send, recv_sem=pair_recv,
        device_id={"sub": 1 - s}, device_id_type=MESH,
    )
    pair.start()
    pair.wait_recv()
    crossing = []
    for by in range(1, nm):
        to = (m + by) % nm
        at = pl.multiple_of((2 * to + s) * share, share)
        cross_out[by - 1] = (acc[pl.ds(at, share), :] + pair_in[to].astype(jnp.float32)).astype(jnp.bfloat16)
        copy = pltpu.make_async_remote_copy(
            src_ref=cross_out.at[by - 1], dst_ref=cross_in.at[by - 1],
            send_sem=cross_send.at[by - 1], recv_sem=cross_recv.at[by - 1],
            device_id={"mdl": to}, device_id_type=MESH,
        )
        copy.start()
        crossing.append(copy)
    at = pl.multiple_of((2 * m + s) * share, share)
    total = acc[pl.ds(at, share), :] + pair_in[m].astype(jnp.float32)
    for by in range(1, nm):
        crossing[by - 1].wait_recv()
        total += cross_in[by - 1].astype(jnp.float32)
    out_ref[...] = total
    pair.wait_send()
    for copy in crossing:
        copy.wait_send()


def feed_forward(all_rows, gate_weight, up_weight, down_weight):
    n, nm = lax.axis_size("ctx"), lax.axis_size("mdl")
    rows, depth_in = all_rows.shape
    units = gate_weight.shape[1]
    columns = down_weight.shape[1]
    width = 256
    chunks = units // width
    share = rows // (2 * nm)
    bf, f32 = jnp.bfloat16, jnp.float32
    bufs = 3
    dma = pltpu.SemaphoreType.DMA
    return pl.pallas_call(
        functools.partial(ffn_kernel, n, nm, LAG),
        out_shape=jax.ShapeDtypeStruct((share, columns), f32),
        in_specs=[pl.BlockSpec(memory_space=pltpu.VMEM)] + [pl.BlockSpec(memory_space=pl.ANY)] * 3,
        out_specs=pl.BlockSpec(memory_space=pltpu.VMEM),
        scratch_shapes=[
            pltpu.VMEM((chunks, rows, 2 * width), bf),
            pltpu.VMEM((chunks, rows // 2, 2 * width), bf),
            pltpu.VMEM((chunks, rows // 2, 2 * width), bf),
            pltpu.VMEM((chunks, rows, width), bf),
            pltpu.VMEM((bufs, depth_in, width), bf),
            pltpu.VMEM((bufs, depth_in, width), bf),
            pltpu.VMEM((bufs, width, columns), bf),
            pltpu.VMEM((rows, columns), f32),
            pltpu.VMEM((nm, share, columns), bf),
            pltpu.VMEM((nm, share, columns), bf),
            pltpu.VMEM((nm - 1, share, columns), bf),
            pltpu.VMEM((nm - 1, share, columns), bf),
            dma((bufs,)), dma((bufs,)), dma((bufs,)),
        ] + [dma((chunks,))] * 8 + [dma, dma, dma((nm - 1,)), dma((nm - 1,))],
        compiler_params=pltpu.CompilerParams(
            collective_id=1, has_side_effects=True, vmem_limit_bytes=52 << 20
        ),
        name="feed_forward",
    )(all_rows, gate_weight, up_weight, down_weight)


HEADS = 2
NOT_VISIBLE = -1e30


def attend_kernel(
    n, nm, lag, score_scale, per_group,
    q_ref, kv_ref, bias_ref, residual_ref, out_hbm, hidden_ref, rows_ref,
    q_all, value_t, scores, own, own_stat, sum_lo, sum_hi, stat_lo, stat_hi, attn, out_buf,
    acc, pair_out, pair_in, cross_out, cross_in, projected, squares, gathered,
    out_sem, q_send, q_recv,
    lo_send, lo_recv, hi_send, hi_recv, slo_send, slo_recv, shi_send, shi_recv,
    alo_send, alo_recv, ahi_send, ahi_recv,
    pair_send, pair_recv, cross_send, cross_recv, square_send, square_recv,
    near_send, near_recv, far_send, far_recv,
):
    c = lax.axis_index("ctx")
    m = lax.axis_index("mdl")
    s = lax.axis_index("sub")
    chunks, rows, width = q_all.shape
    half = rows // 2
    block = q_ref.shape[0]
    slots = kv_ref.shape[1]
    head_dim = width // HEADS
    f32, bf = jnp.float32, jnp.bfloat16

    barrier = pltpu.get_barrier_semaphore()
    for by in range(1, n):
        pl.semaphore_signal(barrier, inc=1, device_id={"ctx": (c + by) % n}, device_id_type=MESH)
    pl.semaphore_signal(barrier, inc=1, device_id={"sub": 1 - s}, device_id_type=MESH)
    for by in range(1, nm):
        pl.semaphore_signal(barrier, inc=1, device_id={"mdl": (m + by) % nm}, device_id_type=MESH)

    def out_copy(j):
        at = pl.ds(pl.multiple_of(j * width, width), width)
        return pltpu.make_async_copy(out_hbm.at[at, :], out_buf.at[j], out_sem.at[j])

    def remote(src, dst, send, recv, to):
        return pltpu.make_async_remote_copy(
            src_ref=src, dst_ref=dst, send_sem=send, recv_sem=recv, device_id={"ctx": to}, device_id_type=MESH
        )

    def block_at(index):
        return pl.ds(pl.multiple_of(index * block, block), block)

    def query_copy(j, by):
        return remote(
            q_ref.at[:, pl.ds(j * width, width)], q_all.at[j, block_at(c), :],
            q_send.at[j, by - 1], q_recv.at[j, c], (c + by) % n,
        )

    def query_arrival(j, source):
        piece = q_all.at[j, block_at(source), :]
        return remote(piece, piece, q_send.at[j, 0], q_recv.at[j, source], source)

    for j in range(chunks):
        out_copy(j).start()
    acc[...] = jnp.zeros_like(acc)
    pl.semaphore_wait(barrier, n - 1 + 1 + nm - 1)

    for j in range(chunks):
        for by in range(1, n):
            query_copy(j, by).start()
    for j in range(chunks):
        q_all[j, block_at(c), :] = q_ref[:, j * width:(j + 1) * width]
    for g in range(kv_ref.shape[0]):
        for at in range(0, slots, 512):
            value_t[g, :, at:at + 512] = kv_ref[g, at:at + 512, head_dim:].T

    lower = (c + n - 1) % n
    upper = (c + 1) % n
    lo_rows, hi_rows = pl.ds(0, half), pl.ds(half, half)

    def lo_copies(j, first):
        return (
            remote(own.at[j, 0] if first else sum_lo.at[j], sum_lo.at[j], lo_send.at[j], lo_recv.at[j], lower),
            remote(own_stat.at[j, 0] if first else stat_lo.at[j], stat_lo.at[j], slo_send.at[j], slo_recv.at[j], lower),
        )

    def hi_copies(j, first):
        return (
            remote(own.at[j, 1] if first else sum_hi.at[j], sum_hi.at[j], hi_send.at[j], hi_recv.at[j], upper),
            remote(own_stat.at[j, 1] if first else stat_hi.at[j], stat_hi.at[j], shi_send.at[j], shi_recv.at[j], upper),
        )

    def attn_lo(j):
        return remote(attn.at[j, lo_rows], attn.at[j, lo_rows], alo_send.at[j], alo_recv.at[j], upper)

    def attn_hi(j):
        return remote(attn.at[j, hi_rows], attn.at[j, hi_rows], ahi_send.at[j], ahi_recv.at[j], lower)

    def valid(j):
        return jnp.logical_and(j >= 0, j < chunks)

    def merged(j, side, came, came_stat):
        result = []
        for h in range(HEADS):
            at = slice(h * head_dim, (h + 1) * head_dim)
            max_a, max_b = came_stat[j, h:h + 1, :], own_stat[j, side, h:h + 1, :]
            sum_a = came_stat[j, HEADS + h:HEADS + h + 1, :]
            sum_b = own_stat[j, side, HEADS + h:HEADS + h + 1, :]
            top = jnp.maximum(max_a, max_b)
            weight_a, weight_b = jnp.exp2(max_a - top), jnp.exp2(max_b - top)
            result.append((
                top,
                weight_a * sum_a + weight_b * sum_b,
                weight_a * came[j, at, :].astype(f32) + weight_b * own[j, side, at, :].astype(f32),
            ))
        return result

    def put(j, state, to, to_stat):
        for h, (top, total, weighted) in enumerate(state):
            to[j, h * head_dim:(h + 1) * head_dim, :] = weighted.astype(bf)
            to_stat[j, h:h + 1, :] = top
            to_stat[j, HEADS + h:HEADS + h + 1, :] = total

    def finish(j, state, first_row):
        for h, (_, total, weighted) in enumerate(state):
            attn[j, first_row:first_row + half, h * head_dim:(h + 1) * head_dim] = (weighted / total).T.astype(bf)

    span = 512

    def attend(j):
        group = j * HEADS // per_group
        spans = range(0, slots, span)

        def score(h, at, top):
            part = lax.dot_general(
                kv_ref[group, at:at + span, :head_dim], q_all[j, :, h * head_dim:(h + 1) * head_dim],
                (((1,), (1,)), ((), ())), preferred_element_type=f32,
            ) * score_scale + bias_ref[at:at + span, :]
            scores[h, at:at + span, :] = part
            return jnp.maximum(top, jnp.max(part, axis=0, keepdims=True))

        def weigh(h, at, top, total, weighted):
            prob = jnp.exp2(scores[h, at:at + span, :] - top)
            total += jnp.sum(prob, axis=0, keepdims=True)
            weighted += jnp.dot(value_t[group, :, at:at + span], prob.astype(bf), preferred_element_type=f32)
            return total, weighted

        lowest = jnp.full((1, rows), NOT_VISIBLE, f32)
        top = lowest
        for at in spans:
            top = score(0, at, top)
        for h in range(HEADS):
            next_top = lowest
            total, weighted = jnp.zeros((1, rows), f32), jnp.zeros((head_dim, rows), f32)
            for at in spans:
                if h + 1 < HEADS:
                    next_top = score(h + 1, at, next_top)
                total, weighted = weigh(h, at, top, total, weighted)
            for side in range(2):
                lanes = slice(side * half, (side + 1) * half)
                own[j, side, h * head_dim:(h + 1) * head_dim, :] = weighted[:, lanes].astype(bf)
                own_stat[j, side, h:h + 1, :] = top[:, lanes]
                own_stat[j, side, HEADS + h:HEADS + h + 1, :] = total[:, lanes]
            top = next_top

    own_stat[...] = jnp.zeros_like(own_stat)

    def step(t, carry):
        @pl.when(t < chunks)
        def _():
            for by in range(1, n):
                query_arrival(t, (c + by) % n).wait_recv()
            attend(t)

        a = t - lag * (n - 1 - c)

        @pl.when(jnp.logical_and(valid(a), c == n - 1))
        def _():
            for copy in lo_copies(a, True):
                copy.start()

        @pl.when(jnp.logical_and(valid(a), c < n - 1))
        def _():
            for copy in lo_copies(a, False):
                copy.wait_recv()
            state = merged(a, 0, sum_lo, stat_lo)

            @pl.when(c > 0)
            def _():
                put(a, state, sum_lo, stat_lo)
                for copy in lo_copies(a, False):
                    copy.start()

            @pl.when(c == 0)
            def _():
                finish(a, state, 0)
                attn_lo(a).start()

        b = t - lag * c

        @pl.when(jnp.logical_and(valid(b), c == 0))
        def _():
            for copy in hi_copies(b, True):
                copy.start()

        @pl.when(jnp.logical_and(valid(b), c > 0))
        def _():
            for copy in hi_copies(b, False):
                copy.wait_recv()
            state = merged(b, 1, sum_hi, stat_hi)

            @pl.when(c < n - 1)
            def _():
                put(b, state, sum_hi, stat_hi)
                for copy in hi_copies(b, False):
                    copy.start()

            @pl.when(c == n - 1)
            def _():
                finish(b, state, half)
                attn_hi(b).start()

        ha = t - lag * (n - 1) - lag * c

        @pl.when(jnp.logical_and(valid(ha), c > 0))
        def _():
            attn_lo(ha).wait_recv()

            @pl.when(c < n - 1)
            def _():
                attn_lo(ha).start()

        hb = t - lag * (n - 1) - lag * (n - 1 - c)

        @pl.when(jnp.logical_and(valid(hb), c < n - 1))
        def _():
            attn_hi(hb).wait_recv()

            @pl.when(c > 0)
            def _():
                attn_hi(hb).start()

        d = t - 2 * lag * (n - 1)

        @pl.when(valid(d))
        def _():
            out_copy(d).wait()
            acc[...] += jnp.dot(attn[d], out_buf[d], preferred_element_type=f32)

        return carry

    lax.fori_loop(0, chunks + 2 * lag * (n - 1), step, 0)

    sum_over_heads(nm, m, s, acc, pair_out, pair_in, cross_out, cross_in,
                   pair_send, pair_recv, cross_send, cross_recv, projected)

    share = hidden_ref.shape[0]
    hidden = residual_ref[...].astype(f32) + projected[...]
    hidden_ref[...] = hidden
    squares[c] = jnp.broadcast_to(jnp.sum(hidden * hidden, axis=1, keepdims=True), squares.shape[1:])
    for by in range(1, n):
        remote(squares.at[c], squares.at[c], square_send.at[by - 1], square_recv.at[c], (c + by) % n).start()
    for by in range(1, n):
        source = (c + by) % n
        remote(squares.at[source], squares.at[source], square_send.at[by - 1], square_recv.at[source], source).wait_recv()
    square_sum = jnp.sum(squares[...], axis=0)[:, :1]
    mine = 2 * m + s
    gathered[mine] = (hidden_ref[...] * lax.rsqrt(square_sum / D + 1e-05)).astype(bf)

    def to_mdl(index, by, recv, to):
        return pltpu.make_async_remote_copy(
            src_ref=gathered.at[index], dst_ref=gathered.at[index], send_sem=far_send.at[by - 1],
            recv_sem=recv, device_id={"mdl": to}, device_id_type=MESH,
        )

    def to_sub(k, index):
        return pltpu.make_async_remote_copy(
            src_ref=gathered.at[index], dst_ref=gathered.at[index], send_sem=near_send.at[k],
            recv_sem=near_recv.at[k], device_id={"sub": 1 - s}, device_id_type=MESH,
        )

    for by in range(1, nm):
        to_mdl(mine, by, far_recv.at[m], (m + by) % nm).start()
    to_sub(m, mine).start()
    for by in range(1, nm):
        k = (m + by) % nm
        to_mdl(2 * k + s, by, far_recv.at[k], k).wait_recv()
        to_sub(k, 2 * k + s).start()
    for k in range(nm):
        to_sub(k, 2 * k + 1 - s).wait_recv()
    for index in range(2 * nm):
        rows_ref[index * share:(index + 1) * share, :] = gathered[index]

    for by in range(1, nm):
        to_mdl(mine, by, far_recv.at[m], (m + by) % nm).wait_send()
    for k in range(nm):
        to_sub(k, 2 * k + s).wait_send()
    for by in range(1, n):
        remote(squares.at[c], squares.at[c], square_send.at[by - 1], square_recv.at[c], (c + by) % n).wait_send()
    for j in range(chunks):
        for by in range(1, n):
            query_copy(j, by).wait_send()

    def drain(j, carry):
        @pl.when(c == n - 1)
        def _():
            for copy in lo_copies(j, True):
                copy.wait_send()

        @pl.when(jnp.logical_and(c > 0, c < n - 1))
        def _():
            for copy in lo_copies(j, False) + hi_copies(j, False):
                copy.wait_send()

        @pl.when(c == 0)
        def _():
            for copy in hi_copies(j, True):
                copy.wait_send()

        @pl.when(c < n - 1)
        def _():
            attn_lo(j).wait_send()

        @pl.when(c > 0)
        def _():
            attn_hi(j).wait_send()

        return carry

    lax.fori_loop(0, chunks, drain, 0)


def attend_and_project(queries, cache_slots, bias, residual, out_weight):
    n, nm = lax.axis_size("ctx"), lax.axis_size("mdl")
    block, heads_width = queries.shape
    slots, group_heads, both = cache_slots.shape
    head_dim = both // 2
    width = HEADS * head_dim
    chunks = heads_width // width
    per_group = heads_width // head_dim // group_heads
    rows = block * n
    half = rows // 2
    share, columns = residual.shape
    bf, f32 = jnp.bfloat16, jnp.float32
    dma = pltpu.SemaphoreType.DMA
    vmem = pl.BlockSpec(memory_space=pltpu.VMEM)
    return pl.pallas_call(
        functools.partial(attend_kernel, n, nm, LAG, head_dim ** (-0.5) * LOG2_E, per_group),
        out_shape=(
            jax.ShapeDtypeStruct((share, columns), f32),
            jax.ShapeDtypeStruct((rows, columns), bf),
        ),
        in_specs=[vmem] * 4 + [pl.BlockSpec(memory_space=pl.ANY)],
        out_specs=(vmem, vmem),
        scratch_shapes=[
            pltpu.VMEM((chunks, rows, width), bf),
            pltpu.VMEM((group_heads, head_dim, slots), bf),
            pltpu.VMEM((HEADS, slots, rows), f32),
            pltpu.VMEM((chunks, 2, width, half), bf),
            pltpu.VMEM((chunks, 2, 8, half), f32),
            pltpu.VMEM((chunks, width, half), bf),
            pltpu.VMEM((chunks, width, half), bf),
            pltpu.VMEM((chunks, 8, half), f32),
            pltpu.VMEM((chunks, 8, half), f32),
            pltpu.VMEM((chunks, rows, width), bf),
            pltpu.VMEM((chunks, width, columns), bf),
            pltpu.VMEM((rows, columns), f32),
            pltpu.VMEM((nm, share, columns), bf),
            pltpu.VMEM((nm, share, columns), bf),
            pltpu.VMEM((nm - 1, share, columns), bf),
            pltpu.VMEM((nm - 1, share, columns), bf),
            pltpu.VMEM((share, columns), f32),
            pltpu.VMEM((n, share, 128), f32),
            pltpu.VMEM((2 * nm, share, columns), bf),
            dma((chunks,)), dma((chunks, n - 1)), dma((chunks, n)),
        ] + [dma((chunks,))] * 12 + [
            dma, dma, dma((nm - 1,)), dma((nm - 1,)), dma((n - 1,)), dma((n,)),
            dma((nm,)), dma((nm,)), dma((nm - 1,)), dma((nm,)),
        ],
        compiler_params=pltpu.CompilerParams(
            collective_id=2, has_side_effects=True, vmem_limit_bytes=52 << 20
        ),
        name="attend",
    )(queries, jnp.transpose(cache_slots, (1, 0, 2)), bias, residual, out_weight)


PARTS = 2
HOPS = (2, 4)
HOP2 = 3
RING = 7 * HOP2 + 4
QUERY_GROUPS = 2
STAT_ROWS = 16
SEND_AT = (0, 1)
PASS_AT = (4, 6)
GAP = 0
STAGES = (0, 1, 2, 3, 4, 8)


def block_kernel(
    n, nm, score_scale, per_group, width_total,
    position_ref, fill_ref, end_ref, q_ref, kv_ref, residual_ref, out_hbm, gate_hbm, up_hbm, down_hbm,
    hidden_ref, out_ref,
    bias, q_all, value_t, scores, tops, own_a, in_a, mid_a, attn, out_buf, acc_a,
    x_all, square, scale,
    own, sum_lo, sum_hi, hid, gate_buf, up_buf, down_buf, acc,
    pair_out, pair_in, cross_out, cross_in,
    out_sem, q_send, q_recv, q_pass, in_send, in_recv, mid_send, mid_recv,
    ax_send, ax_recv, near_a_send, near_a_recv, far_a_send, far_a_recv,
    pair_send, pair_recv, cross_send, cross_recv, square_send, square_recv,
    gx_send, gx_recv, gs_send, gs_recv,
    gate_sem, up_sem, down_sem,
    lo_send, lo_recv, hi_send, hi_recv, hlo_send, hlo_recv, hhi_send, hhi_recv,
):
    c = lax.axis_index("ctx")
    m = lax.axis_index("mdl")
    s = lax.axis_index("sub")
    f32, bf = jnp.float32, jnp.bfloat16
    items, _, rows, head_dim = attn.shape
    pair_width = HEADS * head_dim
    heads = items // PARTS
    group_heads = heads // QUERY_GROUPS
    group_width = group_heads * pair_width
    slots = kv_ref.shape[1]
    piece = rows // n
    share = rows // (2 * nm)
    mine = 2 * m + s

    barrier = pltpu.get_barrier_semaphore()
    for by in range(1, n):
        pl.semaphore_signal(barrier, inc=1, device_id={"ctx": (c + by) % n}, device_id_type=MESH)
    pl.semaphore_signal(barrier, inc=1, device_id={"sub": 1 - s}, device_id_type=MESH)
    for by in range(1, nm):
        pl.semaphore_signal(barrier, inc=1, device_id={"mdl": (m + by) % nm}, device_id_type=MESH)

    def remote(src, dst, send, recv, to, axis="ctx"):
        return pltpu.make_async_remote_copy(
            src_ref=src, dst_ref=dst, send_sem=send, recv_sem=recv, device_id={axis: to}, device_id_type=MESH
        )

    def out_copy(j):
        at = pl.ds(pl.multiple_of(j * pair_width, pair_width), pair_width)
        return pltpu.make_async_copy(out_hbm.at[at, :], out_buf.at[j], out_sem.at[j])

    width = hid.shape[2]
    chunks = gate_hbm.shape[1] // width
    units = PARTS * chunks
    depth = gate_buf.shape[0]

    def gate_copy(i):
        at = pl.ds(pl.multiple_of((i % chunks) * width, width), width)
        return (
            pltpu.make_async_copy(gate_hbm.at[:, at], gate_buf.at[i % depth], gate_sem.at[i % depth]),
            pltpu.make_async_copy(up_hbm.at[:, at], up_buf.at[i % depth], up_sem.at[i % depth]),
        )

    def down_copy(i):
        at = pl.ds(pl.multiple_of((i % chunks) * width, width), width)
        return pltpu.make_async_copy(down_hbm.at[at, :], down_buf.at[i % depth], down_sem.at[i % depth])

    def piece_at(index):
        return pl.ds(pl.multiple_of(index * piece, piece), piece)

    left = c < n // 2
    inner = jnp.where(left, c + 1, c - 1)
    outer = jnp.where(left, jnp.maximum(c - 1, 0), jnp.minimum(c + 1, n - 1))
    end = jnp.logical_or(c == 0, c == n - 1)
    middle = jnp.logical_not(end)
    keep = jnp.where(left, 0, 1)
    give = 1 - keep
    far = n - 1 - outer

    def query_copy(p, k, by):
        return remote(
            q_ref.at[p * piece:(p + 1) * piece, k * group_width:(k + 1) * group_width], q_all.at[p, k, piece_at(c), :],
            q_send.at[p, k, by - 1], q_recv.at[p, k, c], (c + by) % n,
        )

    def direct(by):
        return jnp.logical_or(middle, (c + by) % n != n - 1 - c)

    def send_queries(p, k):
        for by in (2, 1, 3):
            pl.when(direct(by))(query_copy(p, k, by).start)

    def drain_queries(p, k):
        for by in range(1, n):
            pl.when(direct(by))(query_copy(p, k, by).wait_send)
        pl.when(middle)(query_pass(p, k).wait_send)

    def query_arrival(p, k, source):
        there = q_all.at[p, k, piece_at(source), :]
        return remote(there, there, q_send.at[p, k, 0], q_recv.at[p, k, source], source)

    def query_pass(p, k):
        there = q_all.at[p, k, piece_at(far), :]
        return remote(there, there, q_pass.at[p, k], q_recv.at[p, k, far], outer)

    def pass_queries(p, k):
        @pl.when(middle)
        def _():
            query_arrival(p, k, far).wait_recv()
            query_pass(p, k).start()

    def wait_queries(p, k):
        for by in range(1, n):
            source = (c + by) % n
            pl.when(jnp.logical_or(end, source != far))(query_arrival(p, k, source).wait_recv)

    pl.semaphore_wait(barrier, n - 1 + 1 + nm - 1)
    for k in range(QUERY_GROUPS):
        send_queries(0, k)
    for j in range(heads):
        out_copy(j).start()
    for p in range(PARTS):
        for k in range(QUERY_GROUPS):
            q_all[p, k, piece_at(c), :] = q_ref[p * piece:(p + 1) * piece, k * group_width:(k + 1) * group_width]
    for i in range(depth - 1):
        for copy in gate_copy(i):
            copy.start()
        down_copy(i).start()

    fill = fill_ref[0]
    row = lax.broadcasted_iota(jnp.int32, (1, rows), 1)
    image = ((row // share) * (PARTS * share) + row % share) // IMG_TOK
    limits = jnp.zeros((1, rows), jnp.int32)
    for k in range(IMAGES):
        limits = jnp.where(image == k, end_ref[k], limits)
    lane = lax.broadcasted_iota(jnp.int32, (1, 128), 1)
    for k in range(slots // 128):
        tags = jnp.where(lane + k * 128 < fill, position_ref[k:k + 1, :], 2**30).astype(f32)
        column = jnp.broadcast_to(tags, (128, 128)).T[:, :1]
        bias[k * 128:(k + 1) * 128, :] = jnp.where(column <= limits.astype(f32), 0.0, NOT_VISIBLE)
    for g in range(kv_ref.shape[0]):
        for at in range(0, slots, 512):
            value_t[g, :, at:at + 512] = kv_ref[g, at:at + 512, head_dim:].T
    acc_a[...] = jnp.zeros_like(acc_a)
    acc[...] = jnp.zeros_like(acc)

    def split(x, count):
        terms = []
        for _ in range(count):
            terms.append(x.astype(bf).astype(f32))
            x = x - terms[-1]
        return terms

    def put_partial(ref, at, top, total, weighted):
        ref[(*at, slice(0, head_dim), slice(None))] = weighted.astype(bf)
        terms = (*split(top, 3), *split(total, 2))
        line = lax.broadcasted_iota(jnp.int32, (STAT_ROWS, rows), 0)
        stat = jnp.zeros((STAT_ROWS, rows), f32)
        for k, term in enumerate(terms):
            stat = jnp.where(line == k, term, stat)
        ref[(*at, slice(head_dim, head_dim + STAT_ROWS), slice(None))] = stat.astype(bf)

    def merged(partials):
        stats = [x[head_dim:].astype(f32) for x in partials]
        tops_in = [stat[0:1] + stat[1:2] + stat[2:3] for stat in stats]
        top = functools.reduce(jnp.maximum, tops_in)
        total, weighted = 0.0, 0.0
        for x, stat, top_in in zip(partials, stats, tops_in):
            weight = jnp.exp2(top_in - top)
            total += weight * (stat[3:4] + stat[4:5])
            weighted += weight * x[:head_dim].astype(f32)
        return top, total, weighted

    span = 512
    spans = range(0, slots, span)
    both = HEADS * rows

    def group_of(i):
        return ((i % heads) * HEADS) // per_group

    def score(i, slot, at, top):
        j = i % heads
        base = (j % group_heads) * pair_width
        q = jnp.concatenate([
            q_all[i // heads, j // group_heads, :, pl.ds(pl.multiple_of(base + h * head_dim, head_dim), head_dim)]
            for h in range(HEADS)
        ], axis=0)
        part = lax.dot_general(
            kv_ref[group_of(i), at:at + span, :head_dim], q, (((1,), (1,)), ((), ())), preferred_element_type=f32,
        ) * score_scale + jnp.concatenate([bias[at:at + span, :]] * HEADS, axis=1)
        scores[slot, at:at + span, :] = part
        return jnp.maximum(top, jnp.max(part, axis=0, keepdims=True))

    def weigh(i, slot, at, top, total, weighted):
        prob = jnp.exp2(scores[slot, at:at + span, :] - top)
        total += jnp.sum(prob, axis=0, keepdims=True)
        weighted += jnp.dot(value_t[group_of(i), :, at:at + span], prob.astype(bf), preferred_element_type=f32)
        return total, weighted

    def score_first(i, slot):
        top = jnp.full((1, both), NOT_VISIBLE, f32)
        for at in spans:
            top = score(i, slot, at, top)
        tops[slot, 0:1, :] = top

    def attend(i, slot, more):
        top = tops[slot, 0:1, :]
        next_top = jnp.full((1, both), NOT_VISIBLE, f32)
        total, weighted = jnp.zeros((1, both), f32), jnp.zeros((head_dim, both), f32)
        for at in spans:
            if more:
                next_top = score(i + 1, 1 - slot, at, next_top)
            total, weighted = weigh(i, slot, at, top, total, weighted)
        if more:
            tops[1 - slot, 0:1, :] = next_top
        for h in range(HEADS):
            lanes = slice(h * rows, (h + 1) * rows)
            put_partial(own_a, (i, h), top[:, lanes], total[:, lanes], weighted[:, lanes])

    def inward(i):
        return remote(own_a.at[i], in_a.at[i], in_send.at[i], in_recv.at[i], inner)

    def across(i):
        return remote(in_a.at[i, give], mid_a.at[i], mid_send.at[i], mid_recv.at[i], inner)

    def attn_across(i, h):
        return remote(attn.at[i, h], attn.at[i, h], ax_send.at[i], ax_recv.at[i], inner)

    def attn_near(i, h, to):
        return remote(attn.at[i, h], attn.at[i, h], near_a_send.at[i], near_a_recv.at[i], to)

    def attn_far(i, h, to):
        return remote(attn.at[i, h], attn.at[i, h], far_a_send.at[i], far_a_recv.at[i], to)

    def valid(i, count):
        return jnp.logical_and(i >= 0, i < count)

    def pair_copy(e):
        return remote(pair_out.at[e], pair_in.at[e], pair_send.at[e], pair_recv.at[e], 1 - s, "sub")

    def cross_copy(e, by):
        return remote(
            cross_out.at[e, by - 1], cross_in.at[e, by - 1], cross_send.at[e, by - 1], cross_recv.at[e, by - 1],
            (m + by) % nm, "mdl",
        )

    def sum_pair(e, source, p):
        for k in range(nm):
            at = pl.multiple_of((2 * k + 1 - s) * share, share)
            pair_out[e, k] = source[p, pl.ds(at, share), :].astype(bf)
        pair_copy(e).start()

    def sum_cross(e, source, p):
        pair_copy(e).wait_recv()
        for by in range(1, nm):
            to = (m + by) % nm
            at = pl.multiple_of((2 * to + s) * share, share)
            cross_out[e, by - 1] = (source[p, pl.ds(at, share), :] + pair_in[e, to].astype(f32)).astype(bf)
            cross_copy(e, by).start()

    def sum_total(e, source, p):
        at = pl.multiple_of(mine * share, share)
        total = source[p, pl.ds(at, share), :] + pair_in[e, m].astype(f32)
        for by in range(1, nm):
            cross_copy(e, by).wait_recv()
            total += cross_in[e, by - 1].astype(f32)
        return total

    def sum_drain(e):
        pair_copy(e).wait_send()
        for by in range(1, nm):
            cross_copy(e, by).wait_send()

    def share_at(index):
        return pl.ds(pl.multiple_of(index * share, share), share)

    def to_mdl(p, index, by, recv, to):
        there = x_all.at[p, share_at(index), :]
        return remote(there, there, gx_send.at[p, by - 1], recv, to, "mdl")

    def to_sub(p, k, index):
        there = x_all.at[p, share_at(index), :]
        return remote(there, there, gs_send.at[p, k], gs_recv.at[p, k], 1 - s, "sub")

    def square_copy(p, by):
        return remote(square.at[p, c], square.at[p, c], square_send.at[p, by - 1], square_recv.at[p, c], (c + by) % n)

    def stream_rows(p):
        hidden = residual_ref[p * share:(p + 1) * share, :].astype(f32) + sum_total(p, acc_a, p)
        hidden_ref[p * share:(p + 1) * share, :] = hidden
        x_all[p, share_at(mine), :] = hidden.astype(bf)
        for by in range(1, nm):
            to_mdl(p, mine, by, gx_recv.at[p, m], (m + by) % nm).start()
        to_sub(p, m, mine).start()

    def stream_pass(p):
        for by in range(1, nm):
            k = (m + by) % nm
            to_mdl(p, 2 * k + s, by, gx_recv.at[p, k], k).wait_recv()
            to_sub(p, k, 2 * k + s).start()

    def stream_done(p):
        for k in range(nm):
            to_sub(p, k, 2 * k + 1 - s).wait_recv()
        x = x_all[p].astype(f32)
        total = jnp.sum(x * x, axis=1, keepdims=True)
        square[p, c] = jnp.broadcast_to(total, (rows, 128)).T[:8, :]
        for by in range(1, n):
            square_copy(p, by).start()

    def row_scale(p):
        for by in range(1, n):
            source = (c + by) % n
            remote(
                square.at[p, source], square.at[p, source], square_send.at[p, by - 1], square_recv.at[p, source], source
            ).wait_recv()
        mean = jnp.sum(square[p], axis=0)[:1, :] / width_total
        scale[p] = jnp.broadcast_to(lax.rsqrt(mean + 1e-05), (128, rows)).T

    def stream_drain(p):
        for by in range(1, nm):
            to_mdl(p, mine, by, gx_recv.at[p, m], (m + by) % nm).wait_send()
        for k in range(nm):
            to_sub(p, k, 2 * k + s).wait_send()
        for by in range(1, n):
            square_copy(p, by).wait_send()

    for k in range(QUERY_GROUPS):
        pass_queries(0, k)
    wait_queries(0, 0)
    score_first(0, 0)

    def drain_attention(i):
        pl.when(end)(inward(i).wait_send)

        @pl.when(middle)
        def _():
            across(i).wait_send()
            attn_across(i, keep).wait_send()
            attn_near(i, keep, outer).wait_send()
            attn_far(i, give, outer).wait_send()

    later = heads + GAP
    attends = items + GAP
    ready = (heads - 1 + n * HOPS[0], attends - 1 + n * HOPS[1])
    first_unit = ready[0] + STAGES[4] + 1
    attended = ready[1] + 2

    def item_at(t, hops=0, after=0):
        early, late = t - hops * HOPS[0] - after, t - hops * HOPS[1] - after
        return jnp.where(early < heads, early, jnp.where(late < later, -1, late - GAP))

    def attention_compute(t, slot):
        i = item_at(t)
        for k in range(1, QUERY_GROUPS):
            for p, start in ((0, 0), (1, later)):
                pl.when(t + 1 == start + k * group_heads)(functools.partial(wait_queries, p, k))

        @pl.when(jnp.logical_or(t < heads - 1, jnp.logical_and(t >= later, t < attends - 1)))
        def _():
            attend(i, slot, True)

        for ends_at, begins_at in ((heads - 1, None), (attends - 1, None), (None, later - 1)):
            if ends_at is not None and ends_at % 2 == slot:
                @pl.when(t == ends_at)
                def _():
                    attend(i, slot, False)

            if begins_at is not None and begins_at % 2 == slot:
                @pl.when(t == begins_at)
                def _():
                    wait_queries(1, 0)
                    score_first(heads, 1 - slot)

    def attention_step(t):
        for k in range(QUERY_GROUPS):
            pl.when(t == SEND_AT[k])(functools.partial(send_queries, 1, k))
            pl.when(t == PASS_AT[k])(functools.partial(pass_queries, 1, k))

        sent = item_at(t)

        @pl.when(jnp.logical_and(end, valid(sent, items)))
        def _():
            inward(sent).start()

        a = item_at(t, 1)

        @pl.when(jnp.logical_and(middle, valid(a, items)))
        def _():
            inward(a).wait_recv()
            put_partial(in_a, (a, give), *merged([own_a[a, give], in_a[a, give]]))
            across(a).start()

        b = item_at(t, 2)

        @pl.when(jnp.logical_and(middle, valid(b, items)))
        def _():
            across(b).wait_recv()
            _, total, weighted = merged([own_a[b, keep], in_a[b, keep], mid_a[b]])
            attn[b, keep] = (weighted / total).T.astype(bf)
            attn_across(b, keep).start()
            attn_near(b, keep, outer).start()

        g = item_at(t, 3)

        @pl.when(jnp.logical_and(middle, valid(g, items)))
        def _():
            attn_across(g, give).wait_recv()
            attn_far(g, give, outer).start()

        d = item_at(t, n)

        @pl.when(valid(d, items))
        def _():
            @pl.when(end)
            def _():
                attn_near(d, keep, inner).wait_recv()
                attn_far(d, give, inner).wait_recv()

            @pl.when(d < heads)
            def _():
                out_copy(d).wait()

            p = d // heads
            both_heads = jnp.concatenate([attn[d, h] for h in range(HEADS)], axis=1)
            acc_a[p] += jnp.dot(both_heads, out_buf[d % heads], preferred_element_type=f32)

        done = item_at(t, n, 1)

        @pl.when(valid(done, items))
        def _():
            drain_attention(done)

    def stage_step(t):
        for p in range(PARTS):
            for at, stage in zip(STAGES, (
                lambda p: sum_pair(p, acc_a, p), lambda p: sum_cross(p, acc_a, p), stream_rows, stream_pass, stream_done, row_scale,
            )):
                pl.when(t == ready[p] + at)(functools.partial(stage, p))

    lower = (c + n - 1) % n
    upper = (c + 1) % n
    half = rows // 2
    lo_rows, hi_rows = pl.ds(0, half), pl.ds(half, half)

    def lo_first(i):
        r = i % RING
        return remote(own.at[r, lo_rows], sum_lo.at[r], lo_send.at[r], lo_recv.at[r], lower)

    def lo_next(i):
        r = i % RING
        return remote(sum_lo.at[r], sum_lo.at[r], lo_send.at[r], lo_recv.at[r], lower)

    def hi_first(i):
        r = i % RING
        return remote(own.at[r, hi_rows], sum_hi.at[r], hi_send.at[r], hi_recv.at[r], upper)

    def hi_next(i):
        r = i % RING
        return remote(sum_hi.at[r], sum_hi.at[r], hi_send.at[r], hi_recv.at[r], upper)

    def hid_lo(i):
        r = i % RING
        return remote(hid.at[r, lo_rows], hid.at[r, lo_rows], hlo_send.at[r], hlo_recv.at[r], upper)

    def hid_hi(i):
        r = i % RING
        return remote(hid.at[r, hi_rows], hid.at[r, hi_rows], hhi_send.at[r], hhi_recv.at[r], lower)

    def activated(total, i, first):
        by_row = scale[i // chunks, first:first + half, :1]
        gate, up = total[:, :width] * by_row, total[:, width:] * by_row
        return (gate / (1.0 + jnp.exp(-gate)) * up).astype(bf)

    def drain_units(i):
        @pl.when(c == n - 1)
        def _():
            lo_first(i).wait_send()

        @pl.when(jnp.logical_and(c > 0, c < n - 1))
        def _():
            lo_next(i).wait_send()
            hi_next(i).wait_send()

        @pl.when(c == 0)
        def _():
            hi_first(i).wait_send()

        @pl.when(c < n - 1)
        def _():
            hid_lo(i).wait_send()

        @pl.when(c > 0)
        def _():
            hid_hi(i).wait_send()

    turn = HOP2 * (n - 1)

    def unit_step(t):
        @pl.when(t < units)
        def _():
            for copy in gate_copy(t):
                copy.wait()

            @pl.when(t + depth - 1 < units)
            def _():
                for copy in gate_copy(t + depth - 1):
                    copy.start()

            x = x_all[t // chunks]
            own[t % RING, :, :width] = jnp.dot(x, gate_buf[t % depth], preferred_element_type=f32).astype(bf)
            own[t % RING, :, width:] = jnp.dot(x, up_buf[t % depth], preferred_element_type=f32).astype(bf)

        a = t - HOP2 * (n - 1 - c)

        @pl.when(jnp.logical_and(valid(a, units), c == n - 1))
        def _():
            lo_first(a).start()

        @pl.when(jnp.logical_and(valid(a, units), c < n - 1))
        def _():
            lo_next(a).wait_recv()
            total = sum_lo[a % RING].astype(f32) + own[a % RING, :half].astype(f32)

            @pl.when(c > 0)
            def _():
                sum_lo[a % RING] = total.astype(bf)
                lo_next(a).start()

            @pl.when(c == 0)
            def _():
                hid[a % RING, :half] = activated(total, a, 0)
                hid_lo(a).start()

        b = t - HOP2 * c

        @pl.when(jnp.logical_and(valid(b, units), c == 0))
        def _():
            hi_first(b).start()

        @pl.when(jnp.logical_and(valid(b, units), c > 0))
        def _():
            hi_next(b).wait_recv()
            total = sum_hi[b % RING].astype(f32) + own[b % RING, half:].astype(f32)

            @pl.when(c < n - 1)
            def _():
                sum_hi[b % RING] = total.astype(bf)
                hi_next(b).start()

            @pl.when(c == n - 1)
            def _():
                hid[b % RING, half:] = activated(total, b, half)
                hid_hi(b).start()

        ha = t - turn - HOP2 * c

        @pl.when(jnp.logical_and(valid(ha, units), c > 0))
        def _():
            hid_lo(ha).wait_recv()

            @pl.when(c < n - 1)
            def _():
                hid_lo(ha).start()

        hb = t - turn - HOP2 * (n - 1 - c)

        @pl.when(jnp.logical_and(valid(hb, units), c < n - 1))
        def _():
            hid_hi(hb).wait_recv()

            @pl.when(c > 0)
            def _():
                hid_hi(hb).start()

        d = t - 2 * turn

        @pl.when(valid(d, units))
        def _():
            down_copy(d).wait()

            @pl.when(d + depth - 1 < units)
            def _():
                down_copy(d + depth - 1).start()

            acc[d // chunks] += jnp.dot(hid[d % RING], down_buf[d % depth], preferred_element_type=f32)

        @pl.when(valid(d - 1, units))
        def _():
            drain_units(d - 1)

        def first_out():
            out_ref[0:share, :] = sum_total(2, acc, 0)

        for k, stage in enumerate((lambda: sum_pair(2, acc, 0), lambda: sum_cross(2, acc, 0), first_out)):
            pl.when(d == chunks + 2 * k)(stage)

    def attention_only(u, carry):
        for slot in range(2):
            attention_compute(2 * u + slot, slot)
            attention_step(2 * u + slot)
            stage_step(2 * u + slot)
        return carry

    def attention_and_units(t, carry):
        attention_step(t)
        stage_step(t)
        unit_step(t - first_unit)
        return carry

    def units_only(t, carry):
        stage_step(t)
        unit_step(t - first_unit)
        return carry

    assert first_unit % 2 == 0 and first_unit >= attends and GAP % 2 == 0 and HOPS[0] <= HOPS[1]
    assert ready[1] + STAGES[5] < first_unit + chunks
    lax.fori_loop(0, first_unit // 2, attention_only, 0)
    lax.fori_loop(first_unit, attended, attention_and_units, 0)
    lax.fori_loop(attended, first_unit + units + 2 * turn, units_only, 0)

    sum_pair(3, acc, 1)
    drain_units(units - 1)
    for p in range(PARTS):
        for k in range(QUERY_GROUPS):
            drain_queries(p, k)
    for p in range(PARTS):
        stream_drain(p)
    for e in range(3):
        sum_drain(e)
    sum_cross(3, acc, 1)
    out_ref[share:2 * share, :] = sum_total(3, acc, 1)
    sum_drain(3)


def whole_block(
    queries, cache_slots, slot_position, shard_fill, image_end, residual, out_weight, gate_weight, up_weight, down_weight
):
    n, nm = lax.axis_size("ctx"), lax.axis_size("mdl")
    block, heads_width = queries.shape
    slots, group_heads, kv_width = cache_slots.shape
    head_dim = kv_width // 2
    pair_width = HEADS * head_dim
    heads = heads_width // pair_width
    items = PARTS * heads
    per_group = heads_width // head_dim // group_heads
    rows = block * n // PARTS
    half = rows // 2
    columns = residual.shape[1]
    share = rows // (2 * nm)
    width = 256
    bufs = 3
    bf, f32 = jnp.bfloat16, jnp.float32
    dma = pltpu.SemaphoreType.DMA
    vmem = pl.BlockSpec(memory_space=pltpu.VMEM)
    smem = pl.BlockSpec(memory_space=pltpu.SMEM)
    sums = 2 * PARTS
    return pl.pallas_call(
        functools.partial(block_kernel, n, nm, head_dim ** (-0.5) * LOG2_E, per_group, n * columns),
        out_shape=(
            jax.ShapeDtypeStruct((PARTS * share, columns), f32),
            jax.ShapeDtypeStruct((PARTS * share, columns), f32),
        ),
        in_specs=[vmem, smem, smem, vmem, vmem, vmem] + [pl.BlockSpec(memory_space=pl.ANY)] * 4,
        out_specs=(vmem, vmem),
        scratch_shapes=[
            pltpu.VMEM((slots, rows), f32),
            pltpu.VMEM((PARTS, QUERY_GROUPS, rows, heads_width // QUERY_GROUPS), bf),
            pltpu.VMEM((group_heads, head_dim, slots), bf),
            pltpu.VMEM((2, slots, HEADS * rows), f32),
            pltpu.VMEM((2, 8, HEADS * rows), f32),
            pltpu.VMEM((items, HEADS, head_dim + STAT_ROWS, rows), bf),
            pltpu.VMEM((items, HEADS, head_dim + STAT_ROWS, rows), bf),
            pltpu.VMEM((items, head_dim + STAT_ROWS, rows), bf),
            pltpu.VMEM((items, HEADS, rows, head_dim), bf),
            pltpu.VMEM((heads, pair_width, columns), bf),
            pltpu.VMEM((PARTS, rows, columns), f32),
            pltpu.VMEM((PARTS, rows, columns), bf),
            pltpu.VMEM((PARTS, n, 8, rows), f32),
            pltpu.VMEM((PARTS, rows, 128), f32),
            pltpu.VMEM((RING, rows, 2 * width), bf),
            pltpu.VMEM((RING, half, 2 * width), bf),
            pltpu.VMEM((RING, half, 2 * width), bf),
            pltpu.VMEM((RING, rows, width), bf),
            pltpu.VMEM((bufs, columns, width), bf),
            pltpu.VMEM((bufs, columns, width), bf),
            pltpu.VMEM((bufs, width, columns), bf),
            pltpu.VMEM((PARTS, rows, columns), f32),
            pltpu.VMEM((sums, nm, share, columns), bf),
            pltpu.VMEM((sums, nm, share, columns), bf),
            pltpu.VMEM((sums, nm - 1, share, columns), bf),
            pltpu.VMEM((sums, nm - 1, share, columns), bf),
            dma((heads,)), dma((PARTS, QUERY_GROUPS, n - 1)), dma((PARTS, QUERY_GROUPS, n)), dma((PARTS, QUERY_GROUPS)),
        ] + [dma((items,))] * 10 + [
            dma((sums,)), dma((sums,)), dma((sums, nm - 1)), dma((sums, nm - 1)), dma((PARTS, n - 1)), dma((PARTS, n)),
            dma((PARTS, nm - 1)), dma((PARTS, nm)), dma((PARTS, nm)), dma((PARTS, nm)),
            dma((bufs,)), dma((bufs,)), dma((bufs,)),
        ] + [dma((RING,))] * 8,
        compiler_params=pltpu.CompilerParams(
            collective_id=3, has_side_effects=True, vmem_limit_bytes=47 << 20
        ),
        name="block",
    )(
        slot_position.reshape(slots // 128, 128), shard_fill, image_end, queries,
        jnp.transpose(cache_slots, (1, 0, 2)), residual, out_weight, gate_weight, up_weight, down_weight,
    )


def fits_parts(queries, residual, n, nm):
    block, share = queries.shape[0], residual.shape[0]
    return n == 4 and block == share and block % (16 * PARTS) == 0 and IMG_TOK % block == 0 and block * n == PARTS * 128


def body(
    queries,
    cache_slots,
    slot_position,
    shard_fill,
    image_end,
    residual,
    out_weight,
    gate_weight,
    up_weight,
    down_weight,
):
    if fits_parts(queries, residual, lax.axis_size("ctx"), lax.axis_size("mdl")):
        return whole_block(
            queries, cache_slots, slot_position, shard_fill, image_end,
            residual, out_weight, gate_weight, up_weight, down_weight,
        )
    slot_index = jnp.arange(cache_slots.shape[0], dtype=jnp.int32)
    slot_tags = jnp.where(slot_index < shard_fill[0], slot_position, 2**30)
    limits = visible_limits(image_end, 0, queries.shape[0] * lax.axis_size("ctx"))
    bias = jnp.where(slot_tags[:, None] <= limits[None, :], 0.0, NOT_VISIBLE).astype(jnp.float32)
    hidden_state, all_rows = attend_and_project(queries, cache_slots, bias, residual, out_weight)
    forward_delta = feed_forward(all_rows, gate_weight, up_weight, down_weight)
    return (hidden_state, forward_delta)


def solution(mesh):
    in_specs = (
        P(("grp", "ctx"), ("mdl", "sub")),
        P(("grp", "ctx"), ("mdl", "sub"), None),
        P(("grp", "ctx")),
        P(("grp", "ctx")),
        P("grp"),
        P(("grp", "mdl", "sub"), "ctx"),
        P(("mdl", "sub"), "ctx"),
        P("ctx", ("mdl", "sub")),
        P("ctx", ("mdl", "sub")),
        P(("mdl", "sub"), "ctx"),
    )
    out_specs = (P(("grp", "mdl", "sub"), "ctx"), P(("grp", "mdl", "sub"), "ctx"))
    return jax.shard_map(body, mesh=mesh, in_specs=in_specs, out_specs=out_specs, check_vma=False)
```

```python
import functools

import jax
import jax.numpy as jnp
from jax import lax
from jax.experimental import pallas as pl
from jax.experimental.pallas import tpu as pltpu
from jax.sharding import PartitionSpec as P

D = 8192
IMAGES = 2
IMG_TOK = 128
LOG2_E = 1.4426950408889634


def visible_limits(image_end, first_row, query_count):
    row_index = first_row + jnp.arange(query_count, dtype=jnp.int32)
    image_index = row_index // IMG_TOK
    matches = image_index[:, None] == jnp.arange(IMAGES, dtype=jnp.int32)[None, :]
    return jnp.sum(jnp.where(matches, image_end[None, :], 0), axis=1)


MESH = pl.DeviceIdType.MESH
LAG = 3


def ffn_kernel(
    n, nm, lag, x_ref, gate_hbm, up_hbm, down_hbm, out_ref,
    own, sum_lo, sum_hi, hid, gate_buf, up_buf, down_buf, acc, pair_out, pair_in, cross_out, cross_in,
    gate_sem, up_sem, down_sem,
    lo_send, lo_recv, hi_send, hi_recv, hlo_send, hlo_recv, hhi_send, hhi_recv,
    pair_send, pair_recv, cross_send, cross_recv,
):
    c = lax.axis_index("ctx")
    m = lax.axis_index("mdl")
    s = lax.axis_index("sub")
    chunks = own.shape[0]
    rows = x_ref.shape[0]
    half = rows // 2
    width = hid.shape[2]
    depth = gate_buf.shape[0]

    barrier = pltpu.get_barrier_semaphore()
    for by in (1, n - 1):
        pl.semaphore_signal(barrier, inc=1, device_id={"ctx": (c + by) % n}, device_id_type=MESH)
    pl.semaphore_signal(barrier, inc=1, device_id={"sub": 1 - s}, device_id_type=MESH)
    for by in range(1, nm):
        pl.semaphore_signal(barrier, inc=1, device_id={"mdl": (m + by) % nm}, device_id_type=MESH)

    def gate_copy(j):
        at = pl.ds(pl.multiple_of(j * width, width), width)
        return (
            pltpu.make_async_copy(gate_hbm.at[:, at], gate_buf.at[j % depth], gate_sem.at[j % depth]),
            pltpu.make_async_copy(up_hbm.at[:, at], up_buf.at[j % depth], up_sem.at[j % depth]),
        )

    def down_copy(j):
        at = pl.ds(pl.multiple_of(j * width, width), width)
        return pltpu.make_async_copy(down_hbm.at[at, :], down_buf.at[j % depth], down_sem.at[j % depth])

    def remote(src, dst, send, recv, to):
        return pltpu.make_async_remote_copy(
            src_ref=src, dst_ref=dst, send_sem=send, recv_sem=recv, device_id={"ctx": to}, device_id_type=MESH
        )

    lower = (c + n - 1) % n
    upper = (c + 1) % n
    lo_rows, hi_rows = pl.ds(0, half), pl.ds(half, half)

    def lo_first(j):
        return remote(own.at[j, lo_rows], sum_lo.at[j], lo_send.at[j], lo_recv.at[j], lower)

    def lo_next(j):
        return remote(sum_lo.at[j], sum_lo.at[j], lo_send.at[j], lo_recv.at[j], lower)

    def hi_first(j):
        return remote(own.at[j, hi_rows], sum_hi.at[j], hi_send.at[j], hi_recv.at[j], upper)

    def hi_next(j):
        return remote(sum_hi.at[j], sum_hi.at[j], hi_send.at[j], hi_recv.at[j], upper)

    def hid_lo(j):
        return remote(hid.at[j, lo_rows], hid.at[j, lo_rows], hlo_send.at[j], hlo_recv.at[j], upper)

    def hid_hi(j):
        return remote(hid.at[j, hi_rows], hid.at[j, hi_rows], hhi_send.at[j], hhi_recv.at[j], lower)

    for j in range(min(depth - 1, chunks)):
        for copy in gate_copy(j):
            copy.start()
        down_copy(j).start()
    acc[...] = jnp.zeros_like(acc)
    pl.semaphore_wait(barrier, 2 + 1 + nm - 1)

    def valid(j):
        return jnp.logical_and(j >= 0, j < chunks)

    def activated(total):
        gate, up = total[:, :width], total[:, width:]
        return (gate / (1.0 + jnp.exp(-gate)) * up).astype(jnp.bfloat16)

    def step(t, carry):
        @pl.when(t < chunks)
        def _():
            for copy in gate_copy(t):
                copy.wait()

            @pl.when(t + depth - 1 < chunks)
            def _():
                for copy in gate_copy(t + depth - 1):
                    copy.start()

            x = x_ref[...]
            own[t, :, :width] = jnp.dot(
                x, gate_buf[t % depth], preferred_element_type=jnp.float32
            ).astype(jnp.bfloat16)
            own[t, :, width:] = jnp.dot(
                x, up_buf[t % depth], preferred_element_type=jnp.float32
            ).astype(jnp.bfloat16)

        a = t - lag * (n - 1 - c)

        @pl.when(jnp.logical_and(valid(a), c == n - 1))
        def _():
            lo_first(a).start()

        @pl.when(jnp.logical_and(valid(a), c < n - 1))
        def _():
            lo_next(a).wait_recv()
            total = sum_lo[a].astype(jnp.float32) + own[a, :half].astype(jnp.float32)

            @pl.when(c > 0)
            def _():
                sum_lo[a] = total.astype(jnp.bfloat16)
                lo_next(a).start()

            @pl.when(c == 0)
            def _():
                hid[a, :half] = activated(total)
                hid_lo(a).start()

        b = t - lag * c

        @pl.when(jnp.logical_and(valid(b), c == 0))
        def _():
            hi_first(b).start()

        @pl.when(jnp.logical_and(valid(b), c > 0))
        def _():
            hi_next(b).wait_recv()
            total = sum_hi[b].astype(jnp.float32) + own[b, half:].astype(jnp.float32)

            @pl.when(c < n - 1)
            def _():
                sum_hi[b] = total.astype(jnp.bfloat16)
                hi_next(b).start()

            @pl.when(c == n - 1)
            def _():
                hid[b, half:] = activated(total)
                hid_hi(b).start()

        ha = t - lag * (n - 1) - lag * c

        @pl.when(jnp.logical_and(valid(ha), c > 0))
        def _():
            hid_lo(ha).wait_recv()

            @pl.when(c < n - 1)
            def _():
                hid_lo(ha).start()

        hb = t - lag * (n - 1) - lag * (n - 1 - c)

        @pl.when(jnp.logical_and(valid(hb), c < n - 1))
        def _():
            hid_hi(hb).wait_recv()

            @pl.when(c > 0)
            def _():
                hid_hi(hb).start()

        d = t - 2 * lag * (n - 1)

        @pl.when(valid(d))
        def _():
            down_copy(d).wait()

            @pl.when(d + depth - 1 < chunks)
            def _():
                down_copy(d + depth - 1).start()

            acc[...] += jnp.dot(hid[d], down_buf[d % depth], preferred_element_type=jnp.float32)

        return carry

    lax.fori_loop(0, chunks + 2 * lag * (n - 1), step, 0)

    sum_over_heads(nm, m, s, acc, pair_out, pair_in, cross_out, cross_in,
                   pair_send, pair_recv, cross_send, cross_recv, out_ref)

    def drain(j, carry):
        @pl.when(c == n - 1)
        def _():
            lo_first(j).wait_send()

        @pl.when(jnp.logical_and(c > 0, c < n - 1))
        def _():
            lo_next(j).wait_send()
            hi_next(j).wait_send()

        @pl.when(c == 0)
        def _():
            hi_first(j).wait_send()

        @pl.when(c < n - 1)
        def _():
            hid_lo(j).wait_send()

        @pl.when(c > 0)
        def _():
            hid_hi(j).wait_send()

        return carry

    lax.fori_loop(0, chunks, drain, 0)


def sum_over_heads(nm, m, s, acc, pair_out, pair_in, cross_out, cross_in,
                   pair_send, pair_recv, cross_send, cross_recv, out_ref):
    share = out_ref.shape[0]
    for k in range(nm):
        at = pl.multiple_of((2 * k + 1 - s) * share, share)
        pair_out[k] = acc[pl.ds(at, share), :].astype(jnp.bfloat16)
    pair = pltpu.make_async_remote_copy(
        src_ref=pair_out, dst_ref=pair_in, send_sem=pair_send, recv_sem=pair_recv,
        device_id={"sub": 1 - s}, device_id_type=MESH,
    )
    pair.start()
    pair.wait_recv()
    crossing = []
    for by in range(1, nm):
        to = (m + by) % nm
        at = pl.multiple_of((2 * to + s) * share, share)
        cross_out[by - 1] = (acc[pl.ds(at, share), :] + pair_in[to].astype(jnp.float32)).astype(jnp.bfloat16)
        copy = pltpu.make_async_remote_copy(
            src_ref=cross_out.at[by - 1], dst_ref=cross_in.at[by - 1],
            send_sem=cross_send.at[by - 1], recv_sem=cross_recv.at[by - 1],
            device_id={"mdl": to}, device_id_type=MESH,
        )
        copy.start()
        crossing.append(copy)
    at = pl.multiple_of((2 * m + s) * share, share)
    total = acc[pl.ds(at, share), :] + pair_in[m].astype(jnp.float32)
    for by in range(1, nm):
        crossing[by - 1].wait_recv()
        total += cross_in[by - 1].astype(jnp.float32)
    out_ref[...] = total
    pair.wait_send()
    for copy in crossing:
        copy.wait_send()


def feed_forward(all_rows, gate_weight, up_weight, down_weight):
    n, nm = lax.axis_size("ctx"), lax.axis_size("mdl")
    rows, depth_in = all_rows.shape
    units = gate_weight.shape[1]
    columns = down_weight.shape[1]
    width = 256
    chunks = units // width
    share = rows // (2 * nm)
    bf, f32 = jnp.bfloat16, jnp.float32
    bufs = 3
    dma = pltpu.SemaphoreType.DMA
    return pl.pallas_call(
        functools.partial(ffn_kernel, n, nm, LAG),
        out_shape=jax.ShapeDtypeStruct((share, columns), f32),
        in_specs=[pl.BlockSpec(memory_space=pltpu.VMEM)] + [pl.BlockSpec(memory_space=pl.ANY)] * 3,
        out_specs=pl.BlockSpec(memory_space=pltpu.VMEM),
        scratch_shapes=[
            pltpu.VMEM((chunks, rows, 2 * width), bf),
            pltpu.VMEM((chunks, rows // 2, 2 * width), bf),
            pltpu.VMEM((chunks, rows // 2, 2 * width), bf),
            pltpu.VMEM((chunks, rows, width), bf),
            pltpu.VMEM((bufs, depth_in, width), bf),
            pltpu.VMEM((bufs, depth_in, width), bf),
            pltpu.VMEM((bufs, width, columns), bf),
            pltpu.VMEM((rows, columns), f32),
            pltpu.VMEM((nm, share, columns), bf),
            pltpu.VMEM((nm, share, columns), bf),
            pltpu.VMEM((nm - 1, share, columns), bf),
            pltpu.VMEM((nm - 1, share, columns), bf),
            dma((bufs,)), dma((bufs,)), dma((bufs,)),
        ] + [dma((chunks,))] * 8 + [dma, dma, dma((nm - 1,)), dma((nm - 1,))],
        compiler_params=pltpu.CompilerParams(
            collective_id=1, has_side_effects=True, vmem_limit_bytes=52 << 20
        ),
        name="feed_forward",
    )(all_rows, gate_weight, up_weight, down_weight)


HEADS = 2
NOT_VISIBLE = -1e30


def attend_kernel(
    n, nm, lag, score_scale, per_group,
    q_ref, kv_ref, bias_ref, residual_ref, out_hbm, hidden_ref, rows_ref,
    q_all, value_t, scores, own, own_stat, sum_lo, sum_hi, stat_lo, stat_hi, attn, out_buf,
    acc, pair_out, pair_in, cross_out, cross_in, projected, squares, gathered,
    out_sem, q_send, q_recv,
    lo_send, lo_recv, hi_send, hi_recv, slo_send, slo_recv, shi_send, shi_recv,
    alo_send, alo_recv, ahi_send, ahi_recv,
    pair_send, pair_recv, cross_send, cross_recv, square_send, square_recv,
    near_send, near_recv, far_send, far_recv,
):
    c = lax.axis_index("ctx")
    m = lax.axis_index("mdl")
    s = lax.axis_index("sub")
    chunks, rows, width = q_all.shape
    half = rows // 2
    block = q_ref.shape[0]
    slots = kv_ref.shape[1]
    head_dim = width // HEADS
    f32, bf = jnp.float32, jnp.bfloat16

    barrier = pltpu.get_barrier_semaphore()
    for by in range(1, n):
        pl.semaphore_signal(barrier, inc=1, device_id={"ctx": (c + by) % n}, device_id_type=MESH)
    pl.semaphore_signal(barrier, inc=1, device_id={"sub": 1 - s}, device_id_type=MESH)
    for by in range(1, nm):
        pl.semaphore_signal(barrier, inc=1, device_id={"mdl": (m + by) % nm}, device_id_type=MESH)

    def out_copy(j):
        at = pl.ds(pl.multiple_of(j * width, width), width)
        return pltpu.make_async_copy(out_hbm.at[at, :], out_buf.at[j], out_sem.at[j])

    def remote(src, dst, send, recv, to):
        return pltpu.make_async_remote_copy(
            src_ref=src, dst_ref=dst, send_sem=send, recv_sem=recv, device_id={"ctx": to}, device_id_type=MESH
        )

    def block_at(index):
        return pl.ds(pl.multiple_of(index * block, block), block)

    def query_copy(j, by):
        return remote(
            q_ref.at[:, pl.ds(j * width, width)], q_all.at[j, block_at(c), :],
            q_send.at[j, by - 1], q_recv.at[j, c], (c + by) % n,
        )

    def query_arrival(j, source):
        piece = q_all.at[j, block_at(source), :]
        return remote(piece, piece, q_send.at[j, 0], q_recv.at[j, source], source)

    for j in range(chunks):
        out_copy(j).start()
    acc[...] = jnp.zeros_like(acc)
    pl.semaphore_wait(barrier, n - 1 + 1 + nm - 1)

    for j in range(chunks):
        for by in range(1, n):
            query_copy(j, by).start()
    for j in range(chunks):
        q_all[j, block_at(c), :] = q_ref[:, j * width:(j + 1) * width]
    for g in range(kv_ref.shape[0]):
        for at in range(0, slots, 512):
            value_t[g, :, at:at + 512] = kv_ref[g, at:at + 512, head_dim:].T

    lower = (c + n - 1) % n
    upper = (c + 1) % n
    lo_rows, hi_rows = pl.ds(0, half), pl.ds(half, half)

    def lo_copies(j, first):
        return (
            remote(own.at[j, 0] if first else sum_lo.at[j], sum_lo.at[j], lo_send.at[j], lo_recv.at[j], lower),
            remote(own_stat.at[j, 0] if first else stat_lo.at[j], stat_lo.at[j], slo_send.at[j], slo_recv.at[j], lower),
        )

    def hi_copies(j, first):
        return (
            remote(own.at[j, 1] if first else sum_hi.at[j], sum_hi.at[j], hi_send.at[j], hi_recv.at[j], upper),
            remote(own_stat.at[j, 1] if first else stat_hi.at[j], stat_hi.at[j], shi_send.at[j], shi_recv.at[j], upper),
        )

    def attn_lo(j):
        return remote(attn.at[j, lo_rows], attn.at[j, lo_rows], alo_send.at[j], alo_recv.at[j], upper)

    def attn_hi(j):
        return remote(attn.at[j, hi_rows], attn.at[j, hi_rows], ahi_send.at[j], ahi_recv.at[j], lower)

    def valid(j):
        return jnp.logical_and(j >= 0, j < chunks)

    def merged(j, side, came, came_stat):
        result = []
        for h in range(HEADS):
            at = slice(h * head_dim, (h + 1) * head_dim)
            max_a, max_b = came_stat[j, h:h + 1, :], own_stat[j, side, h:h + 1, :]
            sum_a = came_stat[j, HEADS + h:HEADS + h + 1, :]
            sum_b = own_stat[j, side, HEADS + h:HEADS + h + 1, :]
            top = jnp.maximum(max_a, max_b)
            weight_a, weight_b = jnp.exp2(max_a - top), jnp.exp2(max_b - top)
            result.append((
                top,
                weight_a * sum_a + weight_b * sum_b,
                weight_a * came[j, at, :].astype(f32) + weight_b * own[j, side, at, :].astype(f32),
            ))
        return result

    def put(j, state, to, to_stat):
        for h, (top, total, weighted) in enumerate(state):
            to[j, h * head_dim:(h + 1) * head_dim, :] = weighted.astype(bf)
            to_stat[j, h:h + 1, :] = top
            to_stat[j, HEADS + h:HEADS + h + 1, :] = total

    def finish(j, state, first_row):
        for h, (_, total, weighted) in enumerate(state):
            attn[j, first_row:first_row + half, h * head_dim:(h + 1) * head_dim] = (weighted / total).T.astype(bf)

    span = 512

    def attend(j):
        group = j * HEADS // per_group
        spans = range(0, slots, span)

        def score(h, at, top):
            part = lax.dot_general(
                kv_ref[group, at:at + span, :head_dim], q_all[j, :, h * head_dim:(h + 1) * head_dim],
                (((1,), (1,)), ((), ())), preferred_element_type=f32,
            ) * score_scale + bias_ref[at:at + span, :]
            scores[h, at:at + span, :] = part
            return jnp.maximum(top, jnp.max(part, axis=0, keepdims=True))

        def weigh(h, at, top, total, weighted):
            prob = jnp.exp2(scores[h, at:at + span, :] - top)
            total += jnp.sum(prob, axis=0, keepdims=True)
            weighted += jnp.dot(value_t[group, :, at:at + span], prob.astype(bf), preferred_element_type=f32)
            return total, weighted

        lowest = jnp.full((1, rows), NOT_VISIBLE, f32)
        top = lowest
        for at in spans:
            top = score(0, at, top)
        for h in range(HEADS):
            next_top = lowest
            total, weighted = jnp.zeros((1, rows), f32), jnp.zeros((head_dim, rows), f32)
            for at in spans:
                if h + 1 < HEADS:
                    next_top = score(h + 1, at, next_top)
                total, weighted = weigh(h, at, top, total, weighted)
            for side in range(2):
                lanes = slice(side * half, (side + 1) * half)
                own[j, side, h * head_dim:(h + 1) * head_dim, :] = weighted[:, lanes].astype(bf)
                own_stat[j, side, h:h + 1, :] = top[:, lanes]
                own_stat[j, side, HEADS + h:HEADS + h + 1, :] = total[:, lanes]
            top = next_top

    own_stat[...] = jnp.zeros_like(own_stat)

    def step(t, carry):
        @pl.when(t < chunks)
        def _():
            for by in range(1, n):
                query_arrival(t, (c + by) % n).wait_recv()
            attend(t)

        a = t - lag * (n - 1 - c)

        @pl.when(jnp.logical_and(valid(a), c == n - 1))
        def _():
            for copy in lo_copies(a, True):
                copy.start()

        @pl.when(jnp.logical_and(valid(a), c < n - 1))
        def _():
            for copy in lo_copies(a, False):
                copy.wait_recv()
            state = merged(a, 0, sum_lo, stat_lo)

            @pl.when(c > 0)
            def _():
                put(a, state, sum_lo, stat_lo)
                for copy in lo_copies(a, False):
                    copy.start()

            @pl.when(c == 0)
            def _():
                finish(a, state, 0)
                attn_lo(a).start()

        b = t - lag * c

        @pl.when(jnp.logical_and(valid(b), c == 0))
        def _():
            for copy in hi_copies(b, True):
                copy.start()

        @pl.when(jnp.logical_and(valid(b), c > 0))
        def _():
            for copy in hi_copies(b, False):
                copy.wait_recv()
            state = merged(b, 1, sum_hi, stat_hi)

            @pl.when(c < n - 1)
            def _():
                put(b, state, sum_hi, stat_hi)
                for copy in hi_copies(b, False):
                    copy.start()

            @pl.when(c == n - 1)
            def _():
                finish(b, state, half)
                attn_hi(b).start()

        ha = t - lag * (n - 1) - lag * c

        @pl.when(jnp.logical_and(valid(ha), c > 0))
        def _():
            attn_lo(ha).wait_recv()

            @pl.when(c < n - 1)
            def _():
                attn_lo(ha).start()

        hb = t - lag * (n - 1) - lag * (n - 1 - c)

        @pl.when(jnp.logical_and(valid(hb), c < n - 1))
        def _():
            attn_hi(hb).wait_recv()

            @pl.when(c > 0)
            def _():
                attn_hi(hb).start()

        d = t - 2 * lag * (n - 1)

        @pl.when(valid(d))
        def _():
            out_copy(d).wait()
            acc[...] += jnp.dot(attn[d], out_buf[d], preferred_element_type=f32)

        return carry

    lax.fori_loop(0, chunks + 2 * lag * (n - 1), step, 0)

    sum_over_heads(nm, m, s, acc, pair_out, pair_in, cross_out, cross_in,
                   pair_send, pair_recv, cross_send, cross_recv, projected)

    share = hidden_ref.shape[0]
    hidden = residual_ref[...].astype(f32) + projected[...]
    hidden_ref[...] = hidden
    squares[c] = jnp.broadcast_to(jnp.sum(hidden * hidden, axis=1, keepdims=True), squares.shape[1:])
    for by in range(1, n):
        remote(squares.at[c], squares.at[c], square_send.at[by - 1], square_recv.at[c], (c + by) % n).start()
    for by in range(1, n):
        source = (c + by) % n
        remote(squares.at[source], squares.at[source], square_send.at[by - 1], square_recv.at[source], source).wait_recv()
    square_sum = jnp.sum(squares[...], axis=0)[:, :1]
    mine = 2 * m + s
    gathered[mine] = (hidden_ref[...] * lax.rsqrt(square_sum / D + 1e-05)).astype(bf)

    def to_mdl(index, by, recv, to):
        return pltpu.make_async_remote_copy(
            src_ref=gathered.at[index], dst_ref=gathered.at[index], send_sem=far_send.at[by - 1],
            recv_sem=recv, device_id={"mdl": to}, device_id_type=MESH,
        )

    def to_sub(k, index):
        return pltpu.make_async_remote_copy(
            src_ref=gathered.at[index], dst_ref=gathered.at[index], send_sem=near_send.at[k],
            recv_sem=near_recv.at[k], device_id={"sub": 1 - s}, device_id_type=MESH,
        )

    for by in range(1, nm):
        to_mdl(mine, by, far_recv.at[m], (m + by) % nm).start()
    to_sub(m, mine).start()
    for by in range(1, nm):
        k = (m + by) % nm
        to_mdl(2 * k + s, by, far_recv.at[k], k).wait_recv()
        to_sub(k, 2 * k + s).start()
    for k in range(nm):
        to_sub(k, 2 * k + 1 - s).wait_recv()
    for index in range(2 * nm):
        rows_ref[index * share:(index + 1) * share, :] = gathered[index]

    for by in range(1, nm):
        to_mdl(mine, by, far_recv.at[m], (m + by) % nm).wait_send()
    for k in range(nm):
        to_sub(k, 2 * k + s).wait_send()
    for by in range(1, n):
        remote(squares.at[c], squares.at[c], square_send.at[by - 1], square_recv.at[c], (c + by) % n).wait_send()
    for j in range(chunks):
        for by in range(1, n):
            query_copy(j, by).wait_send()

    def drain(j, carry):
        @pl.when(c == n - 1)
        def _():
            for copy in lo_copies(j, True):
                copy.wait_send()

        @pl.when(jnp.logical_and(c > 0, c < n - 1))
        def _():
            for copy in lo_copies(j, False) + hi_copies(j, False):
                copy.wait_send()

        @pl.when(c == 0)
        def _():
            for copy in hi_copies(j, True):
                copy.wait_send()

        @pl.when(c < n - 1)
        def _():
            attn_lo(j).wait_send()

        @pl.when(c > 0)
        def _():
            attn_hi(j).wait_send()

        return carry

    lax.fori_loop(0, chunks, drain, 0)


def attend_and_project(queries, cache_slots, bias, residual, out_weight):
    n, nm = lax.axis_size("ctx"), lax.axis_size("mdl")
    block, heads_width = queries.shape
    slots, group_heads, both = cache_slots.shape
    head_dim = both // 2
    width = HEADS * head_dim
    chunks = heads_width // width
    per_group = heads_width // head_dim // group_heads
    rows = block * n
    half = rows // 2
    share, columns = residual.shape
    bf, f32 = jnp.bfloat16, jnp.float32
    dma = pltpu.SemaphoreType.DMA
    vmem = pl.BlockSpec(memory_space=pltpu.VMEM)
    return pl.pallas_call(
        functools.partial(attend_kernel, n, nm, LAG, head_dim ** (-0.5) * LOG2_E, per_group),
        out_shape=(
            jax.ShapeDtypeStruct((share, columns), f32),
            jax.ShapeDtypeStruct((rows, columns), bf),
        ),
        in_specs=[vmem] * 4 + [pl.BlockSpec(memory_space=pl.ANY)],
        out_specs=(vmem, vmem),
        scratch_shapes=[
            pltpu.VMEM((chunks, rows, width), bf),
            pltpu.VMEM((group_heads, head_dim, slots), bf),
            pltpu.VMEM((HEADS, slots, rows), f32),
            pltpu.VMEM((chunks, 2, width, half), bf),
            pltpu.VMEM((chunks, 2, 8, half), f32),
            pltpu.VMEM((chunks, width, half), bf),
            pltpu.VMEM((chunks, width, half), bf),
            pltpu.VMEM((chunks, 8, half), f32),
            pltpu.VMEM((chunks, 8, half), f32),
            pltpu.VMEM((chunks, rows, width), bf),
            pltpu.VMEM((chunks, width, columns), bf),
            pltpu.VMEM((rows, columns), f32),
            pltpu.VMEM((nm, share, columns), bf),
            pltpu.VMEM((nm, share, columns), bf),
            pltpu.VMEM((nm - 1, share, columns), bf),
            pltpu.VMEM((nm - 1, share, columns), bf),
            pltpu.VMEM((share, columns), f32),
            pltpu.VMEM((n, share, 128), f32),
            pltpu.VMEM((2 * nm, share, columns), bf),
            dma((chunks,)), dma((chunks, n - 1)), dma((chunks, n)),
        ] + [dma((chunks,))] * 12 + [
            dma, dma, dma((nm - 1,)), dma((nm - 1,)), dma((n - 1,)), dma((n,)),
            dma((nm,)), dma((nm,)), dma((nm - 1,)), dma((nm,)),
        ],
        compiler_params=pltpu.CompilerParams(
            collective_id=2, has_side_effects=True, vmem_limit_bytes=52 << 20
        ),
        name="attend",
    )(queries, jnp.transpose(cache_slots, (1, 0, 2)), bias, residual, out_weight)


PARTS = 2
HOPS = (3, 4)
HOP2 = 3
RING = 7 * HOP2 + 4
QUERY_GROUPS = 2
STAT_ROWS = 16
SEND_AT = (0, 1)
PASS_AT = (4, 6)
GAP = 0
STAGES = (0, 1, 2, 3, 4, 8)


def block_kernel(
    n, nm, score_scale, per_group, width_total,
    position_ref, fill_ref, end_ref, q_ref, kv_ref, residual_ref, out_hbm, gate_hbm, up_hbm, down_hbm,
    hidden_ref, out_ref,
    bias, q_all, value_t, scores, tops, own_a, in_a, mid_a, attn, out_buf, acc_a,
    x_all, square, scale,
    own, sum_lo, sum_hi, hid, gate_buf, up_buf, down_buf, acc,
    pair_out, pair_in, cross_out, cross_in,
    out_sem, q_send, q_recv, q_pass, in_send, in_recv, mid_send, mid_recv,
    ax_send, ax_recv, near_a_send, near_a_recv, far_a_send, far_a_recv,
    pair_send, pair_recv, cross_send, cross_recv, square_send, square_recv,
    gx_send, gx_recv, gs_send, gs_recv,
    gate_sem, up_sem, down_sem,
    lo_send, lo_recv, hi_send, hi_recv, hlo_send, hlo_recv, hhi_send, hhi_recv,
):
    c = lax.axis_index("ctx")
    m = lax.axis_index("mdl")
    s = lax.axis_index("sub")
    f32, bf = jnp.float32, jnp.bfloat16
    items, _, rows, head_dim = attn.shape
    pair_width = HEADS * head_dim
    heads = items // PARTS
    group_heads = heads // QUERY_GROUPS
    group_width = group_heads * pair_width
    slots = kv_ref.shape[1]
    piece = rows // n
    share = rows // (2 * nm)
    mine = 2 * m + s

    barrier = pltpu.get_barrier_semaphore()
    for by in range(1, n):
        pl.semaphore_signal(barrier, inc=1, device_id={"ctx": (c + by) % n}, device_id_type=MESH)
    pl.semaphore_signal(barrier, inc=1, device_id={"sub": 1 - s}, device_id_type=MESH)
    for by in range(1, nm):
        pl.semaphore_signal(barrier, inc=1, device_id={"mdl": (m + by) % nm}, device_id_type=MESH)

    def remote(src, dst, send, recv, to, axis="ctx"):
        return pltpu.make_async_remote_copy(
            src_ref=src, dst_ref=dst, send_sem=send, recv_sem=recv, device_id={axis: to}, device_id_type=MESH
        )

    def out_copy(j):
        at = pl.ds(pl.multiple_of(j * pair_width, pair_width), pair_width)
        return pltpu.make_async_copy(out_hbm.at[at, :], out_buf.at[j], out_sem.at[j])

    width = hid.shape[2]
    chunks = gate_hbm.shape[1] // width
    units = PARTS * chunks
    depth = gate_buf.shape[0]

    def gate_copy(i):
        at = pl.ds(pl.multiple_of((i % chunks) * width, width), width)
        return (
            pltpu.make_async_copy(gate_hbm.at[:, at], gate_buf.at[i % depth], gate_sem.at[i % depth]),
            pltpu.make_async_copy(up_hbm.at[:, at], up_buf.at[i % depth], up_sem.at[i % depth]),
        )

    def down_copy(i):
        at = pl.ds(pl.multiple_of((i % chunks) * width, width), width)
        return pltpu.make_async_copy(down_hbm.at[at, :], down_buf.at[i % depth], down_sem.at[i % depth])

    def piece_at(index):
        return pl.ds(pl.multiple_of(index * piece, piece), piece)

    left = c < n // 2
    inner = jnp.where(left, c + 1, c - 1)
    outer = jnp.where(left, jnp.maximum(c - 1, 0), jnp.minimum(c + 1, n - 1))
    end = jnp.logical_or(c == 0, c == n - 1)
    middle = jnp.logical_not(end)
    keep = jnp.where(left, 0, 1)
    give = 1 - keep
    far = n - 1 - outer

    def query_copy(p, k, by):
        return remote(
            q_ref.at[p * piece:(p + 1) * piece, k * group_width:(k + 1) * group_width], q_all.at[p, k, piece_at(c), :],
            q_send.at[p, k, by - 1], q_recv.at[p, k, c], (c + by) % n,
        )

    def direct(by):
        return jnp.logical_or(middle, (c + by) % n != n - 1 - c)

    def send_queries(p, k):
        for by in (2, 1, 3):
            pl.when(direct(by))(query_copy(p, k, by).start)

    def drain_queries(p, k):
        for by in range(1, n):
            pl.when(direct(by))(query_copy(p, k, by).wait_send)
        pl.when(middle)(query_pass(p, k).wait_send)

    def query_arrival(p, k, source):
        there = q_all.at[p, k, piece_at(source), :]
        return remote(there, there, q_send.at[p, k, 0], q_recv.at[p, k, source], source)

    def query_pass(p, k):
        there = q_all.at[p, k, piece_at(far), :]
        return remote(there, there, q_pass.at[p, k], q_recv.at[p, k, far], outer)

    def pass_queries(p, k):
        @pl.when(middle)
        def _():
            query_arrival(p, k, far).wait_recv()
            query_pass(p, k).start()

    def wait_queries(p, k):
        for by in range(1, n):
            source = (c + by) % n
            pl.when(jnp.logical_or(end, source != far))(query_arrival(p, k, source).wait_recv)

    pl.semaphore_wait(barrier, n - 1 + 1 + nm - 1)
    for k in range(QUERY_GROUPS):
        send_queries(0, k)
    for j in range(heads):
        out_copy(j).start()
    for p in range(PARTS):
        for k in range(QUERY_GROUPS):
            q_all[p, k, piece_at(c), :] = q_ref[p * piece:(p + 1) * piece, k * group_width:(k + 1) * group_width]
    for i in range(depth - 1):
        for copy in gate_copy(i):
            copy.start()
        down_copy(i).start()

    fill = fill_ref[0]
    row = lax.broadcasted_iota(jnp.int32, (1, rows), 1)
    image = ((row // share) * (PARTS * share) + row % share) // IMG_TOK
    limits = jnp.zeros((1, rows), jnp.int32)
    for k in range(IMAGES):
        limits = jnp.where(image == k, end_ref[k], limits)
    lane = lax.broadcasted_iota(jnp.int32, (1, 128), 1)
    for k in range(slots // 128):
        tags = jnp.where(lane + k * 128 < fill, position_ref[k:k + 1, :], 2**30).astype(f32)
        column = jnp.broadcast_to(tags, (128, 128)).T[:, :1]
        bias[k * 128:(k + 1) * 128, :] = jnp.where(column <= limits.astype(f32), 0.0, NOT_VISIBLE)
    for g in range(kv_ref.shape[0]):
        for at in range(0, slots, 512):
            value_t[g, :, at:at + 512] = kv_ref[g, at:at + 512, head_dim:].T
    acc_a[...] = jnp.zeros_like(acc_a)
    acc[...] = jnp.zeros_like(acc)

    def split(x, count):
        terms = []
        for _ in range(count):
            terms.append(x.astype(bf).astype(f32))
            x = x - terms[-1]
        return terms

    def put_partial(ref, at, top, total, weighted):
        ref[(*at, slice(0, head_dim), slice(None))] = weighted.astype(bf)
        terms = (*split(top, 3), *split(total, 2))
        line = lax.broadcasted_iota(jnp.int32, (STAT_ROWS, rows), 0)
        stat = jnp.zeros((STAT_ROWS, rows), f32)
        for k, term in enumerate(terms):
            stat = jnp.where(line == k, term, stat)
        ref[(*at, slice(head_dim, head_dim + STAT_ROWS), slice(None))] = stat.astype(bf)

    def merged(partials):
        stats = [x[head_dim:].astype(f32) for x in partials]
        tops_in = [stat[0:1] + stat[1:2] + stat[2:3] for stat in stats]
        top = functools.reduce(jnp.maximum, tops_in)
        total, weighted = 0.0, 0.0
        for x, stat, top_in in zip(partials, stats, tops_in):
            weight = jnp.exp2(top_in - top)
            total += weight * (stat[3:4] + stat[4:5])
            weighted += weight * x[:head_dim].astype(f32)
        return top, total, weighted

    span = 512
    spans = range(0, slots, span)
    both = HEADS * rows

    def group_of(i):
        return ((i % heads) * HEADS) // per_group

    def score(i, slot, at, top):
        j = i % heads
        base = (j % group_heads) * pair_width
        q = jnp.concatenate([
            q_all[i // heads, j // group_heads, :, pl.ds(pl.multiple_of(base + h * head_dim, head_dim), head_dim)]
            for h in range(HEADS)
        ], axis=0)
        part = lax.dot_general(
            kv_ref[group_of(i), at:at + span, :head_dim], q, (((1,), (1,)), ((), ())), preferred_element_type=f32,
        ) * score_scale + jnp.concatenate([bias[at:at + span, :]] * HEADS, axis=1)
        scores[slot, at:at + span, :] = part
        return jnp.maximum(top, jnp.max(part, axis=0, keepdims=True))

    def weigh(i, slot, at, top, total, weighted):
        prob = jnp.exp2(scores[slot, at:at + span, :] - top)
        total += jnp.sum(prob, axis=0, keepdims=True)
        weighted += jnp.dot(value_t[group_of(i), :, at:at + span], prob.astype(bf), preferred_element_type=f32)
        return total, weighted

    def score_first(i, slot):
        top = jnp.full((1, both), NOT_VISIBLE, f32)
        for at in spans:
            top = score(i, slot, at, top)
        tops[slot, 0:1, :] = top

    def attend(i, slot, more):
        top = tops[slot, 0:1, :]
        next_top = jnp.full((1, both), NOT_VISIBLE, f32)
        total, weighted = jnp.zeros((1, both), f32), jnp.zeros((head_dim, both), f32)
        for at in spans:
            if more:
                next_top = score(i + 1, 1 - slot, at, next_top)
            total, weighted = weigh(i, slot, at, top, total, weighted)
        if more:
            tops[1 - slot, 0:1, :] = next_top
        for h in range(HEADS):
            lanes = slice(h * rows, (h + 1) * rows)
            put_partial(own_a, (i, h), top[:, lanes], total[:, lanes], weighted[:, lanes])

    def inward(i):
        return remote(own_a.at[i], in_a.at[i], in_send.at[i], in_recv.at[i], inner)

    def across(i):
        return remote(in_a.at[i, give], mid_a.at[i], mid_send.at[i], mid_recv.at[i], inner)

    def attn_across(i, h):
        return remote(attn.at[i, h], attn.at[i, h], ax_send.at[i], ax_recv.at[i], inner)

    def attn_near(i, h, to):
        return remote(attn.at[i, h], attn.at[i, h], near_a_send.at[i], near_a_recv.at[i], to)

    def attn_far(i, h, to):
        return remote(attn.at[i, h], attn.at[i, h], far_a_send.at[i], far_a_recv.at[i], to)

    def valid(i, count):
        return jnp.logical_and(i >= 0, i < count)

    def pair_copy(e):
        return remote(pair_out.at[e], pair_in.at[e], pair_send.at[e], pair_recv.at[e], 1 - s, "sub")

    def cross_copy(e, by):
        return remote(
            cross_out.at[e, by - 1], cross_in.at[e, by - 1], cross_send.at[e, by - 1], cross_recv.at[e, by - 1],
            (m + by) % nm, "mdl",
        )

    def sum_pair(e, source, p):
        for k in range(nm):
            at = pl.multiple_of((2 * k + 1 - s) * share, share)
            pair_out[e, k] = source[p, pl.ds(at, share), :].astype(bf)
        pair_copy(e).start()

    def sum_cross(e, source, p):
        pair_copy(e).wait_recv()
        for by in range(1, nm):
            to = (m + by) % nm
            at = pl.multiple_of((2 * to + s) * share, share)
            cross_out[e, by - 1] = (source[p, pl.ds(at, share), :] + pair_in[e, to].astype(f32)).astype(bf)
            cross_copy(e, by).start()

    def sum_total(e, source, p):
        at = pl.multiple_of(mine * share, share)
        total = source[p, pl.ds(at, share), :] + pair_in[e, m].astype(f32)
        for by in range(1, nm):
            cross_copy(e, by).wait_recv()
            total += cross_in[e, by - 1].astype(f32)
        return total

    def sum_drain(e):
        pair_copy(e).wait_send()
        for by in range(1, nm):
            cross_copy(e, by).wait_send()

    def share_at(index):
        return pl.ds(pl.multiple_of(index * share, share), share)

    def to_mdl(p, index, by, recv, to):
        there = x_all.at[p, share_at(index), :]
        return remote(there, there, gx_send.at[p, by - 1], recv, to, "mdl")

    def to_sub(p, k, index):
        there = x_all.at[p, share_at(index), :]
        return remote(there, there, gs_send.at[p, k], gs_recv.at[p, k], 1 - s, "sub")

    def square_copy(p, by):
        return remote(square.at[p, c], square.at[p, c], square_send.at[p, by - 1], square_recv.at[p, c], (c + by) % n)

    def stream_rows(p):
        hidden = residual_ref[p * share:(p + 1) * share, :].astype(f32) + sum_total(p, acc_a, p)
        hidden_ref[p * share:(p + 1) * share, :] = hidden
        x_all[p, share_at(mine), :] = hidden.astype(bf)
        for by in range(1, nm):
            to_mdl(p, mine, by, gx_recv.at[p, m], (m + by) % nm).start()
        to_sub(p, m, mine).start()

    def stream_pass(p):
        for by in range(1, nm):
            k = (m + by) % nm
            to_mdl(p, 2 * k + s, by, gx_recv.at[p, k], k).wait_recv()
            to_sub(p, k, 2 * k + s).start()

    def stream_done(p):
        for k in range(nm):
            to_sub(p, k, 2 * k + 1 - s).wait_recv()
        x = x_all[p].astype(f32)
        total = jnp.sum(x * x, axis=1, keepdims=True)
        square[p, c] = jnp.broadcast_to(total, (rows, 128)).T[:8, :]
        for by in range(1, n):
            square_copy(p, by).start()

    def row_scale(p):
        for by in range(1, n):
            source = (c + by) % n
            remote(
                square.at[p, source], square.at[p, source], square_send.at[p, by - 1], square_recv.at[p, source], source
            ).wait_recv()
        mean = jnp.sum(square[p], axis=0)[:1, :] / width_total
        scale[p] = jnp.broadcast_to(lax.rsqrt(mean + 1e-05), (128, rows)).T

    def stream_drain(p):
        for by in range(1, nm):
            to_mdl(p, mine, by, gx_recv.at[p, m], (m + by) % nm).wait_send()
        for k in range(nm):
            to_sub(p, k, 2 * k + s).wait_send()
        for by in range(1, n):
            square_copy(p, by).wait_send()

    for k in range(QUERY_GROUPS):
        pass_queries(0, k)
    wait_queries(0, 0)
    score_first(0, 0)

    def drain_attention(i):
        pl.when(end)(inward(i).wait_send)

        @pl.when(middle)
        def _():
            across(i).wait_send()
            attn_across(i, keep).wait_send()
            attn_near(i, keep, outer).wait_send()
            attn_far(i, give, outer).wait_send()

    later = heads + GAP
    attends = items + GAP
    ready = (heads - 1 + n * HOPS[0], attends - 1 + n * HOPS[1])
    first_unit = ready[0] + STAGES[4] + 1
    attended = ready[1] + 2

    def item_at(t, hops=0, after=0):
        early, late = t - hops * HOPS[0] - after, t - hops * HOPS[1] - after
        return jnp.where(early < heads, early, jnp.where(late < later, -1, late - GAP))

    def attention_compute(t, slot):
        i = item_at(t)
        for k in range(1, QUERY_GROUPS):
            for p, start in ((0, 0), (1, later)):
                pl.when(t + 1 == start + k * group_heads)(functools.partial(wait_queries, p, k))

        @pl.when(jnp.logical_or(t < heads - 1, jnp.logical_and(t >= later, t < attends - 1)))
        def _():
            attend(i, slot, True)

        for ends_at, begins_at in ((heads - 1, None), (attends - 1, None), (None, later - 1)):
            if ends_at is not None and ends_at % 2 == slot:
                @pl.when(t == ends_at)
                def _():
                    attend(i, slot, False)

            if begins_at is not None and begins_at % 2 == slot:
                @pl.when(t == begins_at)
                def _():
                    wait_queries(1, 0)
                    score_first(heads, 1 - slot)

    def attention_step(t):
        for k in range(QUERY_GROUPS):
            pl.when(t == SEND_AT[k])(functools.partial(send_queries, 1, k))
            pl.when(t == PASS_AT[k])(functools.partial(pass_queries, 1, k))

        sent = item_at(t)

        @pl.when(jnp.logical_and(end, valid(sent, items)))
        def _():
            inward(sent).start()

        a = item_at(t, 1)

        @pl.when(jnp.logical_and(middle, valid(a, items)))
        def _():
            inward(a).wait_recv()
            put_partial(in_a, (a, give), *merged([own_a[a, give], in_a[a, give]]))
            across(a).start()

        b = item_at(t, 2)

        @pl.when(jnp.logical_and(middle, valid(b, items)))
        def _():
            across(b).wait_recv()
            _, total, weighted = merged([own_a[b, keep], in_a[b, keep], mid_a[b]])
            attn[b, keep] = (weighted / total).T.astype(bf)
            attn_across(b, keep).start()
            attn_near(b, keep, outer).start()

        g = item_at(t, 3)

        @pl.when(jnp.logical_and(middle, valid(g, items)))
        def _():
            attn_across(g, give).wait_recv()
            attn_far(g, give, outer).start()

        d = item_at(t, n)

        @pl.when(valid(d, items))
        def _():
            @pl.when(end)
            def _():
                attn_near(d, keep, inner).wait_recv()
                attn_far(d, give, inner).wait_recv()

            @pl.when(d < heads)
            def _():
                out_copy(d).wait()

            p = d // heads
            both_heads = jnp.concatenate([attn[d, h] for h in range(HEADS)], axis=1)
            acc_a[p] += jnp.dot(both_heads, out_buf[d % heads], preferred_element_type=f32)

        done = item_at(t, n, 1)

        @pl.when(valid(done, items))
        def _():
            drain_attention(done)

    def stage_step(t):
        for p in range(PARTS):
            for at, stage in zip(STAGES, (
                lambda p: sum_pair(p, acc_a, p), lambda p: sum_cross(p, acc_a, p), stream_rows, stream_pass, stream_done, row_scale,
            )):
                pl.when(t == ready[p] + at)(functools.partial(stage, p))

    lower = (c + n - 1) % n
    upper = (c + 1) % n
    half = rows // 2
    lo_rows, hi_rows = pl.ds(0, half), pl.ds(half, half)

    def lo_first(i):
        r = i % RING
        return remote(own.at[r, lo_rows], sum_lo.at[r], lo_send.at[r], lo_recv.at[r], lower)

    def lo_next(i):
        r = i % RING
        return remote(sum_lo.at[r], sum_lo.at[r], lo_send.at[r], lo_recv.at[r], lower)

    def hi_first(i):
        r = i % RING
        return remote(own.at[r, hi_rows], sum_hi.at[r], hi_send.at[r], hi_recv.at[r], upper)

    def hi_next(i):
        r = i % RING
        return remote(sum_hi.at[r], sum_hi.at[r], hi_send.at[r], hi_recv.at[r], upper)

    def hid_lo(i):
        r = i % RING
        return remote(hid.at[r, lo_rows], hid.at[r, lo_rows], hlo_send.at[r], hlo_recv.at[r], upper)

    def hid_hi(i):
        r = i % RING
        return remote(hid.at[r, hi_rows], hid.at[r, hi_rows], hhi_send.at[r], hhi_recv.at[r], lower)

    def activated(total, i, first):
        by_row = scale[i // chunks, first:first + half, :1]
        gate, up = total[:, :width] * by_row, total[:, width:] * by_row
        return (gate / (1.0 + jnp.exp(-gate)) * up).astype(bf)

    def drain_units(i):
        @pl.when(c == n - 1)
        def _():
            lo_first(i).wait_send()

        @pl.when(jnp.logical_and(c > 0, c < n - 1))
        def _():
            lo_next(i).wait_send()
            hi_next(i).wait_send()

        @pl.when(c == 0)
        def _():
            hi_first(i).wait_send()

        @pl.when(c < n - 1)
        def _():
            hid_lo(i).wait_send()

        @pl.when(c > 0)
        def _():
            hid_hi(i).wait_send()

    turn = HOP2 * (n - 1)

    def unit_step(t):
        @pl.when(t < units)
        def _():
            for copy in gate_copy(t):
                copy.wait()

            @pl.when(t + depth - 1 < units)
            def _():
                for copy in gate_copy(t + depth - 1):
                    copy.start()

            x = x_all[t // chunks]
            own[t % RING, :, :width] = jnp.dot(x, gate_buf[t % depth], preferred_element_type=f32).astype(bf)
            own[t % RING, :, width:] = jnp.dot(x, up_buf[t % depth], preferred_element_type=f32).astype(bf)

        a = t - HOP2 * (n - 1 - c)

        @pl.when(jnp.logical_and(valid(a, units), c == n - 1))
        def _():
            lo_first(a).start()

        @pl.when(jnp.logical_and(valid(a, units), c < n - 1))
        def _():
            lo_next(a).wait_recv()
            total = sum_lo[a % RING].astype(f32) + own[a % RING, :half].astype(f32)

            @pl.when(c > 0)
            def _():
                sum_lo[a % RING] = total.astype(bf)
                lo_next(a).start()

            @pl.when(c == 0)
            def _():
                hid[a % RING, :half] = activated(total, a, 0)
                hid_lo(a).start()

        b = t - HOP2 * c

        @pl.when(jnp.logical_and(valid(b, units), c == 0))
        def _():
            hi_first(b).start()

        @pl.when(jnp.logical_and(valid(b, units), c > 0))
        def _():
            hi_next(b).wait_recv()
            total = sum_hi[b % RING].astype(f32) + own[b % RING, half:].astype(f32)

            @pl.when(c < n - 1)
            def _():
                sum_hi[b % RING] = total.astype(bf)
                hi_next(b).start()

            @pl.when(c == n - 1)
            def _():
                hid[b % RING, half:] = activated(total, b, half)
                hid_hi(b).start()

        ha = t - turn - HOP2 * c

        @pl.when(jnp.logical_and(valid(ha, units), c > 0))
        def _():
            hid_lo(ha).wait_recv()

            @pl.when(c < n - 1)
            def _():
                hid_lo(ha).start()

        hb = t - turn - HOP2 * (n - 1 - c)

        @pl.when(jnp.logical_and(valid(hb, units), c < n - 1))
        def _():
            hid_hi(hb).wait_recv()

            @pl.when(c > 0)
            def _():
                hid_hi(hb).start()

        d = t - 2 * turn

        @pl.when(valid(d, units))
        def _():
            down_copy(d).wait()

            @pl.when(d + depth - 1 < units)
            def _():
                down_copy(d + depth - 1).start()

            acc[d // chunks] += jnp.dot(hid[d % RING], down_buf[d % depth], preferred_element_type=f32)

        @pl.when(valid(d - 1, units))
        def _():
            drain_units(d - 1)

        def first_out():
            out_ref[0:share, :] = sum_total(2, acc, 0)

        for k, stage in enumerate((lambda: sum_pair(2, acc, 0), lambda: sum_cross(2, acc, 0), first_out)):
            pl.when(d == chunks + 2 * k)(stage)

    def attention_only(u, carry):
        for slot in range(2):
            attention_compute(2 * u + slot, slot)
            attention_step(2 * u + slot)
            stage_step(2 * u + slot)
        return carry

    def attention_and_units(t, carry):
        attention_step(t)
        stage_step(t)
        unit_step(t - first_unit)
        return carry

    def units_only(t, carry):
        stage_step(t)
        unit_step(t - first_unit)
        return carry

    assert first_unit % 2 == 0 and first_unit >= attends and GAP % 2 == 0 and HOPS[0] <= HOPS[1]
    assert ready[1] + STAGES[5] < first_unit + chunks
    lax.fori_loop(0, first_unit // 2, attention_only, 0)
    lax.fori_loop(first_unit, attended, attention_and_units, 0)
    lax.fori_loop(attended, first_unit + units + 2 * turn, units_only, 0)

    sum_pair(3, acc, 1)
    drain_units(units - 1)
    for p in range(PARTS):
        for k in range(QUERY_GROUPS):
            drain_queries(p, k)
    for p in range(PARTS):
        stream_drain(p)
    for e in range(3):
        sum_drain(e)
    sum_cross(3, acc, 1)
    out_ref[share:2 * share, :] = sum_total(3, acc, 1)
    sum_drain(3)


def whole_block(
    queries, cache_slots, slot_position, shard_fill, image_end, residual, out_weight, gate_weight, up_weight, down_weight
):
    n, nm = lax.axis_size("ctx"), lax.axis_size("mdl")
    block, heads_width = queries.shape
    slots, group_heads, kv_width = cache_slots.shape
    head_dim = kv_width // 2
    pair_width = HEADS * head_dim
    heads = heads_width // pair_width
    items = PARTS * heads
    per_group = heads_width // head_dim // group_heads
    rows = block * n // PARTS
    half = rows // 2
    columns = residual.shape[1]
    share = rows // (2 * nm)
    width = 256
    bufs = 3
    bf, f32 = jnp.bfloat16, jnp.float32
    dma = pltpu.SemaphoreType.DMA
    vmem = pl.BlockSpec(memory_space=pltpu.VMEM)
    smem = pl.BlockSpec(memory_space=pltpu.SMEM)
    sums = 2 * PARTS
    return pl.pallas_call(
        functools.partial(block_kernel, n, nm, head_dim ** (-0.5) * LOG2_E, per_group, n * columns),
        out_shape=(
            jax.ShapeDtypeStruct((PARTS * share, columns), f32),
            jax.ShapeDtypeStruct((PARTS * share, columns), f32),
        ),
        in_specs=[vmem, smem, smem, vmem, vmem, vmem] + [pl.BlockSpec(memory_space=pl.ANY)] * 4,
        out_specs=(vmem, vmem),
        scratch_shapes=[
            pltpu.VMEM((slots, rows), f32),
            pltpu.VMEM((PARTS, QUERY_GROUPS, rows, heads_width // QUERY_GROUPS), bf),
            pltpu.VMEM((group_heads, head_dim, slots), bf),
            pltpu.VMEM((2, slots, HEADS * rows), f32),
            pltpu.VMEM((2, 8, HEADS * rows), f32),
            pltpu.VMEM((items, HEADS, head_dim + STAT_ROWS, rows), bf),
            pltpu.VMEM((items, HEADS, head_dim + STAT_ROWS, rows), bf),
            pltpu.VMEM((items, head_dim + STAT_ROWS, rows), bf),
            pltpu.VMEM((items, HEADS, rows, head_dim), bf),
            pltpu.VMEM((heads, pair_width, columns), bf),
            pltpu.VMEM((PARTS, rows, columns), f32),
            pltpu.VMEM((PARTS, rows, columns), bf),
            pltpu.VMEM((PARTS, n, 8, rows), f32),
            pltpu.VMEM((PARTS, rows, 128), f32),
            pltpu.VMEM((RING, rows, 2 * width), bf),
            pltpu.VMEM((RING, half, 2 * width), bf),
            pltpu.VMEM((RING, half, 2 * width), bf),
            pltpu.VMEM((RING, rows, width), bf),
            pltpu.VMEM((bufs, columns, width), bf),
            pltpu.VMEM((bufs, columns, width), bf),
            pltpu.VMEM((bufs, width, columns), bf),
            pltpu.VMEM((PARTS, rows, columns), f32),
            pltpu.VMEM((sums, nm, share, columns), bf),
            pltpu.VMEM((sums, nm, share, columns), bf),
            pltpu.VMEM((sums, nm - 1, share, columns), bf),
            pltpu.VMEM((sums, nm - 1, share, columns), bf),
            dma((heads,)), dma((PARTS, QUERY_GROUPS, n - 1)), dma((PARTS, QUERY_GROUPS, n)), dma((PARTS, QUERY_GROUPS)),
        ] + [dma((items,))] * 10 + [
            dma((sums,)), dma((sums,)), dma((sums, nm - 1)), dma((sums, nm - 1)), dma((PARTS, n - 1)), dma((PARTS, n)),
            dma((PARTS, nm - 1)), dma((PARTS, nm)), dma((PARTS, nm)), dma((PARTS, nm)),
            dma((bufs,)), dma((bufs,)), dma((bufs,)),
        ] + [dma((RING,))] * 8,
        compiler_params=pltpu.CompilerParams(
            collective_id=3, has_side_effects=True, vmem_limit_bytes=47 << 20
        ),
        name="block",
    )(
        slot_position.reshape(slots // 128, 128), shard_fill, image_end, queries,
        jnp.transpose(cache_slots, (1, 0, 2)), residual, out_weight, gate_weight, up_weight, down_weight,
    )


def fits_parts(queries, residual, n, nm):
    block, share = queries.shape[0], residual.shape[0]
    return n == 4 and block == share and block % (16 * PARTS) == 0 and IMG_TOK % block == 0 and block * n == PARTS * 128


def body(
    queries,
    cache_slots,
    slot_position,
    shard_fill,
    image_end,
    residual,
    out_weight,
    gate_weight,
    up_weight,
    down_weight,
):
    if fits_parts(queries, residual, lax.axis_size("ctx"), lax.axis_size("mdl")):
        return whole_block(
            queries, cache_slots, slot_position, shard_fill, image_end,
            residual, out_weight, gate_weight, up_weight, down_weight,
        )
    slot_index = jnp.arange(cache_slots.shape[0], dtype=jnp.int32)
    slot_tags = jnp.where(slot_index < shard_fill[0], slot_position, 2**30)
    limits = visible_limits(image_end, 0, queries.shape[0] * lax.axis_size("ctx"))
    bias = jnp.where(slot_tags[:, None] <= limits[None, :], 0.0, NOT_VISIBLE).astype(jnp.float32)
    hidden_state, all_rows = attend_and_project(queries, cache_slots, bias, residual, out_weight)
    forward_delta = feed_forward(all_rows, gate_weight, up_weight, down_weight)
    return (hidden_state, forward_delta)


def solution(mesh):
    in_specs = (
        P(("grp", "ctx"), ("mdl", "sub")),
        P(("grp", "ctx"), ("mdl", "sub"), None),
        P(("grp", "ctx")),
        P(("grp", "ctx")),
        P("grp"),
        P(("grp", "mdl", "sub"), "ctx"),
        P(("mdl", "sub"), "ctx"),
        P("ctx", ("mdl", "sub")),
        P("ctx", ("mdl", "sub")),
        P(("mdl", "sub"), "ctx"),
    )
    out_specs = (P(("grp", "mdl", "sub"), "ctx"), P(("grp", "mdl", "sub"), "ctx"))
    return jax.shard_map(body, mesh=mesh, in_specs=in_specs, out_specs=out_specs, check_vma=False)
```
